32 devices in a mesh: row: 8 (over z, x), col: 4 (over y, core).
Axes of the slice: x: 2, y: 2, z: 4, core: 2. Of those that a mesh axis runs over, the one named last changes fastest.
Arguments:
- coords: float32 [4, 8, 3, 8, 16], P('col', 'row'), may hold values from 0 to 4
- weights: float32 [4, 8, 8, 16], P('col', 'row'), may hold values from 0.25 to 1
- correction_values: float32 [8, 4, 33, 9, 128], P('row', 'col'), may hold values from -6 to 6
- correction_rows: int32 [8, 4, 33, 128], P('row', 'col'), may hold values from 0 to 63, as said below
- correction_columns: int32 [8, 4, 33, 128], P('row', 'col'), may hold values from 0 to 127
- corr_owner: int32 [8, 4, 33], P('row', 'col'), may hold values from 0 to 31, as said below
- corr_used: int32 [8, 4], P('row', 'col'), may hold values from 24 to 33
- corr_fill: int32 [8, 4, 33], P('row', 'col'), may hold values from 32 to 128, as said below
Outputs:
- matrix: float32 [8, 3, 64, 3, 4, 128], P('row', None, None, None, 'col')
The draws below stay inside these ranges and needn't reach their ends.
Inputs may be any that keep to these rules, and one draw needn't show every extreme that they name: `corr_owner`: A device's live blocks name each owner at most 2 times; every device names one common owner in exactly 2 live blocks. `corr_fill`: pairs beyond a block's fill are padding. Within a block, correction_rows // 16 is the same for all pairs, and so is correction_columns // 16. The block's transposed owner (correction_columns // 16) * 4 + correction_rows // 16 is named by at most 2 live blocks of a device; every device names one common transposed owner in exactly 2 live blocks.
All inputs are finite; a program needn't handle non-finite values.
Results may differ from the reference program's by a relative error of at most 0.0003.
Values sent between devices are 32-bit elements; how exact they have to be, the bound alone decides.
A program may use at most 64 MiB of HBM per device.

```python
import math
import jax
import jax.numpy as jnp
from jax import lax

Q = 8
GROUP_ELEMENTS = 16
CAP = 2
CORRECTION_SLOTS = 33
PAIRS_PER_BLOCK = 128
N_ROW = 8
N_COL = 4


def distribute_owners(key_hot, key_rest):
    device_list = N_ROW * N_COL
    hot_owner = jax.random.randint(key_hot, (), 0, device_list)
    picks = jax.vmap(lambda single: jax.random.permutation(single, device_list - 1))(jax.random.split(key_rest, device_list))
    others = (hot_owner + 1 + picks) % device_list
    return jnp.concatenate([jnp.full((device_list, CAP), hot_owner, jnp.int32), others.astype(jnp.int32)], axis=1)


def correction_plan(key):
    base = jax.random.fold_in(key, 11)
    device_list = N_ROW * N_COL
    random_keys = jax.random.split(base, 9)
    owning_device = distribute_owners(random_keys[0], random_keys[1]).reshape(N_ROW, N_COL, CORRECTION_SLOTS)
    mirror = distribute_owners(random_keys[7], random_keys[8])
    reflected_row = mirror // N_COL
    reflected_column = mirror % N_COL
    used_flags = jax.random.randint(random_keys[2], (device_list,), 3 * CORRECTION_SLOTS // 4, CORRECTION_SLOTS + 1)
    device_full = jax.random.randint(random_keys[3], (), 0, device_list)
    used_flags = jnp.where(jnp.arange(device_list) == device_full, CORRECTION_SLOTS, used_flags).reshape(N_ROW, N_COL)
    fill_count = jax.random.randint(random_keys[4], (device_list, CORRECTION_SLOTS), PAIRS_PER_BLOCK // 4, PAIRS_PER_BLOCK + 1)
    fill_count = fill_count.at[:, 0].set(PAIRS_PER_BLOCK).reshape(N_ROW, N_COL, CORRECTION_SLOTS)
    row_offset = jax.random.randint(random_keys[5], (device_list, CORRECTION_SLOTS, PAIRS_PER_BLOCK), 0, GROUP_ELEMENTS)
    row_offset = row_offset.at[:, :, 0].set(GROUP_ELEMENTS - 1).at[:, :, 1].set(0)
    column_offset = jax.random.randint(random_keys[6], (device_list, CORRECTION_SLOTS, PAIRS_PER_BLOCK), 0, GROUP_ELEMENTS)
    column_offset = column_offset.at[:, :, 0].set(GROUP_ELEMENTS - 1).at[:, :, 1].set(0)
    row_list = (reflected_column[:, :, None] * GROUP_ELEMENTS + row_offset).astype(jnp.int32).reshape(N_ROW, N_COL, CORRECTION_SLOTS, PAIRS_PER_BLOCK)
    column_list = (reflected_row[:, :, None] * GROUP_ELEMENTS + column_offset).astype(jnp.int32).reshape(N_ROW, N_COL, CORRECTION_SLOTS, PAIRS_PER_BLOCK)
    return (owning_device, used_flags, fill_count, row_list, column_list)


def draw_corr_owner(key, part):
    return correction_plan(key)[0]


def draw_corr_used(key, part):
    return correction_plan(key)[1]


def draw_corr_fill(key, part):
    return correction_plan(key)[2]


def draw_correction_rows(key, part):
    return correction_plan(key)[3]


def draw_correction_columns(key, part):
    return correction_plan(key)[4]


def block_levels(key, dims, pieces, least, top_value):
    loudness = 1.0
    for position, blocks in pieces:
        steps = jax.random.uniform(jax.random.fold_in(jax.random.fold_in(key, 6), position), (blocks,), jnp.float32, least / len(pieces), top_value / len(pieces))
        loudness = loudness * jnp.repeat(jnp.exp(steps), dims[position] // blocks).reshape((-1,) + (1,) * (len(dims) - 1 - position))
    return loudness


def gaussian(rng, dims, spread, reach, cuts=(), kind=jnp.bfloat16):
    loudness = block_levels(rng, dims, cuts, -0.22, 0.18) if cuts else 1.0
    drawn = jax.random.normal(rng, dims, jnp.float32) * spread * loudness
    return jnp.minimum(jnp.maximum(drawn, -reach), reach).astype(kind)


def setup_inputs(seed: int = 0) -> dict:
    splits = jax.random.split(jax.random.key(seed), 9)
    coords = jnp.clip(4.0 * jax.random.uniform(splits[0], (N_COL, N_ROW, 3, Q, GROUP_ELEMENTS), jnp.float32) ** block_levels(splits[0], (N_COL, N_ROW, 3, Q, GROUP_ELEMENTS), ((0, 4), (1, 8)), -0.2, 0.2), 0.0, 4.0)
    weights = jnp.clip(jnp.exp(math.log(1.0) - 1.3862944 * jax.random.uniform(splits[1], (N_COL, N_ROW, Q, GROUP_ELEMENTS), jnp.float32) ** block_levels(splits[1], (N_COL, N_ROW, Q, GROUP_ELEMENTS), ((0, 4), (1, 8)), -0.2, 0.2)), 0.25, 1.0)
    correction_values = gaussian(splits[2], (N_ROW, N_COL, CORRECTION_SLOTS, 9, PAIRS_PER_BLOCK), 1.0, 6.0, ((0, 8), (1, 4)), jnp.float32)
    correction_rows = draw_correction_rows(jax.random.fold_in(splits[8], 71), 0)
    correction_columns = draw_correction_columns(jax.random.fold_in(splits[8], 71), 0)
    corr_owner = draw_corr_owner(jax.random.fold_in(splits[8], 71), 0)
    corr_used = draw_corr_used(jax.random.fold_in(splits[8], 71), 0)
    corr_fill = draw_corr_fill(jax.random.fold_in(splits[8], 71), 0)
    return dict(coords=coords, weights=weights, correction_values=correction_values, correction_rows=correction_rows, correction_columns=correction_columns, corr_owner=corr_owner, corr_used=corr_used, corr_fill=corr_fill)


EPS_SQUARED = 0.01
KELVIN_A = 1.0 / (4.0 * math.pi)
KELVIN_B = KELVIN_A / 2.8
ISO_TERM = KELVIN_A - KELVIN_B
SOFT_TERM = KELVIN_A * 0.005
ANI_TERM = KELVIN_B

def kelvin(row_x, row_w, col_x, col_w):
    count_rows = row_x.shape[2]
    count_cols = col_x.shape[2]
    totals = [jnp.zeros((count_rows, count_cols), jnp.float32) for entry in range(6)]
    pair_table = ((0, 0), (1, 1), (2, 2), (0, 1), (0, 2), (1, 2))
    for point in range(row_x.shape[1]):
        delta = row_x[:, point][:, None, :, None] - col_x[:, :, None, :]
        dist_sq = delta[0] * delta[0] + delta[1] * delta[1] + delta[2] * delta[2] + EPS_SQUARED
        inverse = 1.0 / jnp.sqrt(dist_sq)
        cubed = inverse * inverse * inverse
        weight = row_w[point][None, :, None] * col_w[:, None, :]
        isotropic = weight * (ISO_TERM * inverse + SOFT_TERM * cubed)
        directed = weight * (ANI_TERM * cubed)
        for slot, pair in enumerate(pair_table):
            term = directed * delta[pair[0]] * delta[pair[1]]
            if pair[0] == pair[1]:
                term = term + isotropic
            totals[slot] = totals[slot] + lax.optimization_barrier(jnp.sum(term, axis=0))
    layout = ((0, 3, 4), (3, 1, 5), (4, 5, 2))
    stacked = jnp.stack([jnp.stack([totals[entry] for entry in line]) for line in layout])
    return stacked.transpose(0, 2, 1, 3)

def reference(coords, weights, correction_values, correction_rows, correction_columns, corr_owner, corr_used, corr_fill):
    rows_n = N_ROW
    cols_n = N_COL
    row_span = cols_n * GROUP_ELEMENTS
    col_span = rows_n * GROUP_ELEMENTS

    def one_block(index):
        row_group = index // cols_n
        col_group = index % cols_n
        row_pts = jnp.take(coords, row_group, axis=1)
        row_wts = jnp.take(weights, row_group, axis=1)
        col_pts = jnp.take(coords, col_group, axis=0)
        col_wts = jnp.take(weights, col_group, axis=0)
        row_x = row_pts.transpose(1, 2, 0, 3).reshape(3, Q, row_span)
        row_w = row_wts.transpose(1, 0, 2).reshape(Q, row_span)
        col_x = col_pts.transpose(1, 2, 0, 3).reshape(3, Q, col_span)
        col_w = col_wts.transpose(1, 0, 2).reshape(Q, col_span)
        return kelvin(row_x, row_w, col_x, col_w)
    blocks = lax.map(one_block, jnp.arange(rows_n * cols_n, dtype=jnp.int32))
    blocks = blocks.reshape(rows_n, cols_n, 3, row_span, 3, col_span).transpose(0, 2, 3, 4, 1, 5)
    slot_table = jnp.arange(CORRECTION_SLOTS, dtype=jnp.int32)
    active_flags = slot_table[None, None, :] < corr_used[:, :, None]
    keep = active_flags[..., None] & (jnp.arange(PAIRS_PER_BLOCK, dtype=jnp.int32)[None, None, None, :] < corr_fill[..., None])
    value_array = jnp.where(keep[:, :, :, None, :], correction_values, 0.0)
    owner_row = (corr_owner // cols_n)[..., None, None]
    owner_col = (corr_owner % cols_n)[..., None, None]
    row_position = correction_rows[:, :, :, None, :]
    column_position = correction_columns[:, :, :, None, :]
    comp = jnp.arange(9, dtype=jnp.int32)
    first = (comp // 3)[None, None, None, :, None]
    second = (comp % 3)[None, None, None, :, None]
    forward = ((((owner_row * 3 + first) * row_span + row_position) * 3 + second) * cols_n + owner_col) * col_span + column_position
    back_row = column_position // GROUP_ELEMENTS
    back_u = column_position % GROUP_ELEMENTS
    back_g = row_position // GROUP_ELEMENTS
    back_t = row_position % GROUP_ELEMENTS
    backward = ((((back_row * 3 + second) * row_span + owner_col * GROUP_ELEMENTS + back_u) * 3 + first) * cols_n + back_g) * col_span + owner_row * GROUP_ELEMENTS + back_t
    flat = blocks.reshape(-1)
    flat = flat.at[forward.reshape(-1)].add(value_array.reshape(-1))
    flat = flat.at[backward.reshape(-1)].add(value_array.reshape(-1))
    return flat.reshape(blocks.shape)
```

```python
import functools
import math

import jax
import jax.numpy as jnp
from jax import lax
from jax.experimental import pallas as pl
from jax.experimental.pallas import tpu as pltpu
from jax.sharding import PartitionSpec as P

MESH = pl.DeviceIdType.MESH
HIGH = lax.Precision.HIGHEST
CAP = 2
COMPS = 9
SLOTS = 2 * CAP
RECORD = SLOTS * (COMPS + 1)
LANES = 128
GROUP = 4

EPS_SQUARED = 0.01
KELVIN_A = 1.0 / (4.0 * math.pi)
KELVIN_B = KELVIN_A / 2.8
ISO_TERM = KELVIN_A - KELVIN_B
SOFT_TERM = KELVIN_A * 0.005
ANI_TERM = KELVIN_B


def dot(a, b, axes, precision=HIGH):
    return lax.dot_general(
        a, b, (axes, ((), ())), precision=precision, preferred_element_type=jnp.float32
    )


def split(value):
    top = value.astype(jnp.bfloat16)
    return top, value - top.astype(jnp.float32)


def halves(value):
    high, rest = split(value)
    return jnp.concatenate([high, rest.astype(jnp.bfloat16)], axis=0)


def iota(shape, axis):
    return lax.broadcasted_iota(jnp.int32, shape, axis)


def kernel(
    rows_n,
    cols_n,
    coords_hbm,
    weights_hbm,
    values_hbm,
    rows_hbm,
    columns_hbm,
    owner_hbm,
    used_ref,
    fill_hbm,
    out_ref,
    coords_ref,
    weights_ref,
    values_ref,
    rows_ref,
    columns_ref,
    owner_ref,
    fill_ref,
    send,
    recv,
    geo,
    geo_by_row,
    geo_by_col,
    row_geo,
    left,
    small,
    number,
    tiles,
    acc,
    load_sem,
    send_sem,
    recv_sem,
    row_send_sem,
    row_recv_sem,
    col_send_sem,
    col_recv_sem,
):
    my_row = lax.axis_index("row")
    my_col = lax.axis_index("col")
    devices = rows_n * cols_n
    me = my_row * cols_n + my_col
    points, count = coords_ref.shape[-2:]
    row_span = cols_n * count
    live_slots, _, width = rows_hbm.shape
    slots = rows_ref.shape[0]

    lines_n = live_slots * COMPS
    loads = [
        pltpu.make_async_copy(source, target, load_sem.at[k])
        for k, (source, target) in enumerate(
            (
                (coords_hbm, coords_ref),
                (weights_hbm, weights_ref),
                (values_hbm.at[:, 0], values_ref.at[pl.ds(0, lines_n)]),
                (rows_hbm.at[:, 0], rows_ref.at[pl.ds(0, live_slots)]),
                (columns_hbm.at[:, 0], columns_ref.at[pl.ds(0, live_slots)]),
                (owner_hbm, owner_ref),
                (fill_hbm, fill_ref),
            )
        )
    ]
    edge = live_slots // 8 * 8
    rows_ref[edge:slots] = jnp.zeros((slots - edge, width), jnp.int32)
    columns_ref[edge:slots] = jnp.zeros((slots - edge, width), jnp.int32)
    edge = lines_n // 8 * 8
    values_ref[edge : slots * COMPS] = jnp.zeros((slots * COMPS - edge, width), jnp.float32)
    for load in loads:
        load.start()

    barrier = pltpu.get_barrier_semaphore()

    @pl.loop(1, devices)
    def _(k):
        other = (me + k) % devices
        pl.semaphore_signal(
            barrier,
            inc=1,
            device_id=(other // cols_n, other % cols_n),
            device_id_type=MESH,
        )

    for load in loads[:2]:
        load.wait()
    spread = (iota((count, LANES), 1) % count == iota((count, LANES), 0)).astype(jnp.float32)
    at_point = iota((points, LANES), 1) // count == iota((points, LANES), 0)
    lines = []
    for comp in range(4):
        piece = coords_ref[0, 0, comp] if comp < 3 else weights_ref[0, 0]
        wide = dot(piece, spread, ((1,), (0,)))
        lines.append(jnp.sum(jnp.where(at_point, wide, 0.0), axis=0, keepdims=True))
    geo[...] = jnp.concatenate(lines + [jnp.zeros((4, LANES), jnp.float32)], axis=0)
    geo_by_col[0] = geo[...]
    geo_by_row[0] = geo[...]

    def row_copy(k):
        return pltpu.make_async_remote_copy(
            src_ref=geo,
            dst_ref=geo_by_row.at[k],
            send_sem=row_send_sem.at[k],
            recv_sem=row_recv_sem.at[k],
            device_id=((my_row + k) % rows_n, my_col),
            device_id_type=MESH,
        )

    def col_copy(k):
        return pltpu.make_async_remote_copy(
            src_ref=geo,
            dst_ref=geo_by_col.at[k],
            send_sem=col_send_sem.at[k],
            recv_sem=col_recv_sem.at[k],
            device_id=(my_row, (my_col + k) % cols_n),
            device_id_type=MESH,
        )

    for load in loads[2:]:
        load.wait()
    owner = jnp.concatenate([owner_ref[0], jnp.zeros((1, slots - live_slots), jnp.int32)], axis=1)
    fills = jnp.concatenate([fill_ref[0], jnp.zeros((1, slots - live_slots), jnp.int32)], axis=1)
    live = iota((1, slots), 1) < used_ref[0, 0]
    square = (slots, slots)
    diagonal = iota(square, 0) == iota(square, 1)
    fill = jnp.sum(jnp.where(diagonal, fills, 0), axis=1, keepdims=True)
    owner_down = jnp.sum(jnp.where(diagonal, owner, 0), axis=1, keepdims=True)
    row_position = rows_ref[...]
    column_position = columns_ref[...]
    row_group = row_position[:, 0:1] // count
    column_group = column_position[:, 0:1] // count
    mirror_down = column_group * cols_n + row_group
    mirror = jnp.sum(jnp.where(diagonal, mirror_down, 0), axis=0, keepdims=True)
    earlier = (iota(square, 0) < iota(square, 1)).astype(jnp.float32).astype(jnp.bfloat16)
    picks = []
    for target in (owner, mirror):
        named = ((target == iota((devices, slots), 0)) & live).astype(jnp.float32)
        rank = dot(named.astype(jnp.bfloat16), earlier, ((1,), (0,)), None)
        for place in range(CAP):
            picks.append(jnp.where(rank == float(place), named, 0.0))
    pick = jnp.concatenate(picks, axis=0).astype(jnp.bfloat16)
    pick = jnp.concatenate([pick, pick], axis=1)
    valid = iota((slots, width), 1) < fill
    row_inner = row_position % count
    column_inner = column_position % count
    forward = ((row_group * rows_n + column_group) * count + row_inner) * count + column_inner
    back_tile = owner_down % cols_n * rows_n + owner_down // cols_n
    backward = (back_tile * count + column_inner) * count + row_inner
    half = CAP * devices
    places = (
        dot(pick[:half], halves(forward.astype(jnp.float32)), ((1,), (0,)), None),
        dot(pick[half:], halves(backward.astype(jnp.float32)), ((1,), (0,)), None),
    )
    for slot in range(SLOTS):
        lot = places[slot // CAP][slot % CAP * devices : (slot % CAP + 1) * devices]
        send[pl.ds(SLOTS * COMPS + slot, devices, stride=RECORD), :] = lot
    for comp in range(COMPS):
        value = values_ref[pl.ds(comp, slots, stride=COMPS), :]
        sent = dot(pick, halves(jnp.where(valid, value, 0.0)), ((1,), (0,)), None)
        for slot in range(SLOTS):
            line = comp if slot < CAP else comp % 3 * 3 + comp // 3
            send[pl.ds(slot * COMPS + line, devices, stride=RECORD), :] = sent[
                slot * devices : (slot + 1) * devices
            ]

    pl.semaphore_wait(barrier, devices - 1)
    pl.loop(1, cols_n)(lambda k: col_copy(k).start())
    pl.loop(1, rows_n)(lambda k: row_copy(k).start())
    recv[0:RECORD, :] = send[pl.ds(pl.multiple_of(me * RECORD, 8), RECORD), :]

    def block_copy(k):
        other = me ^ k
        return pltpu.make_async_remote_copy(
            src_ref=send.at[pl.ds(pl.multiple_of(other * RECORD, 8), RECORD), :],
            dst_ref=recv.at[pl.ds(pl.multiple_of(k * RECORD, 8), RECORD), :],
            send_sem=send_sem.at[k],
            recv_sem=recv_sem.at[k],
            device_id=(other // cols_n, other % cols_n),
            device_id_type=MESH,
        )

    pl.loop(1, devices)(lambda k: block_copy(k).start())

    pl.loop(1, cols_n)(lambda k: col_copy(k).wait())
    pl.loop(1, rows_n)(lambda k: row_copy(k).wait())

    lane = iota((8, LANES), 1)
    col_tiles = []
    for point in range(points):
        tile = jnp.zeros((8, LANES), jnp.float32)
        for part in range(rows_n):
            held = geo_by_row[(my_row - part + rows_n) % rows_n]
            shift = (part - point) * count % LANES
            if shift:
                held = pltpu.roll(held, shift, 1)
            tile = jnp.where(lane // count == part, held, tile)
        col_tiles.append(tile)
    for part in range(cols_n):
        held = geo_by_col[(my_col - part + cols_n) % cols_n]
        square_tile = jnp.concatenate(
            [held, jnp.zeros((LANES - 8, LANES), jnp.float32)], axis=0
        )
        row_geo[part] = square_tile.T

    @pl.loop(0, row_span // count)
    def _(part):
        def at_row_point(point, totals):
            start = pl.multiple_of(point * count, 8)
            here = [row_geo[part, pl.ds(start + first, 8), :] for first in range(0, count, 8)]
            spread = [
                [jnp.broadcast_to(one[:, comp : comp + 1], (8, LANES)) for comp in range(4)]
                for one in here
            ]
            totals = list(totals)
            for tile in col_tiles:
                bx, by, bz, bw = (tile[comp : comp + 1] for comp in range(4))
                for piece, (ax, ay, az, aw) in enumerate(spread):
                    xx, yy, xy, xz, yz, near, soft = totals[piece]
                    dx = ax - bx
                    dy = ay - by
                    dz = az - bz
                    inverse = lax.rsqrt(dx * dx + dy * dy + (dz * dz + EPS_SQUARED))
                    scaled = aw * bw * inverse
                    cubed = scaled * (inverse * inverse)
                    ex = cubed * dx
                    ey = cubed * dy
                    totals[piece] = (
                        xx + ex * dx,
                        yy + ey * dy,
                        xy + ex * dy,
                        xz + ex * dz,
                        yz + ey * dz,
                        near + scaled,
                        soft + cubed,
                    )
            return tuple(totals)

        zero = jnp.zeros((8, LANES), jnp.float32)
        totals = lax.fori_loop(0, points, at_row_point, ((zero,) * 7,) * (count // 8))
        for piece, (xx, yy, xy, xz, yz, near, soft) in enumerate(totals):
            zz = near - EPS_SQUARED * soft - xx - yy
            even = ISO_TERM * near + SOFT_TERM * soft
            xy, xz, yz = (ANI_TERM * term for term in (xy, xz, yz))
            xx, yy, zz = (ANI_TERM * term + even for term in (xx, yy, zz))
            for line, entry in enumerate((xx, xy, xz, xy, yy, yz, xz, yz, zz)):
                start = line // 3 * (row_span * 3) + part * (count * 3) + piece * 24 + line % 3
                out_ref[pl.ds(start, 8, stride=3), :] = entry

    lots = GROUP * SLOTS
    tiles_n = cols_n * rows_n
    acc[...] = jnp.zeros_like(acc)
    small[1] = jnp.zeros_like(small[1])
    number[1] = jnp.zeros_like(number[1])
    down = iota((count, LANES), 0).astype(jnp.float32)
    same = iota((count, lots * count), 1) % count == iota((count, lots * count), 0)
    mine = iota((lots, lots * count), 0) == iota((lots, lots * count), 1) // count

    def squeeze(batch, turn):
        if turn:
            block_copy(batch * GROUP).wait()
        else:
            pl.when(batch > 0)(lambda: block_copy(batch * GROUP).wait())
        for inside in range(1, GROUP):
            block_copy(batch * GROUP + inside).wait()
        records = recv.at[pl.ds(pl.multiple_of(batch * (GROUP * RECORD), 8), GROUP * RECORD), :]
        place = jnp.concatenate(
            [
                records[inside * RECORD + SLOTS * COMPS : (inside + 1) * RECORD]
                for inside in range(GROUP)
            ],
            axis=0,
        )
        whole = jnp.floor(place * (1.0 / (count * count)))
        inner = place - whole * (count * count)
        row_inner = jnp.floor(inner * (1.0 / count))
        column_inner = inner - row_inner * count
        number[turn] = jnp.broadcast_to(
            jnp.sum(jnp.where(mine, whole[:, 0:1], 0.0), axis=0, keepdims=True), number.shape[1:]
        )
        for slot in range(lots):
            first = slot // SLOTS * RECORD + slot % SLOTS * COMPS
            hit = jnp.where(row_inner[slot : slot + 1] == down, 1.0, 0.0).astype(jnp.bfloat16)
            spot = jnp.where(column_inner[slot : slot + 1] == down, 1.0, 0.0).astype(jnp.bfloat16)
            for line in range(COMPS):
                top, rest = split(
                    jnp.broadcast_to(records[first + line : first + line + 1], (count, LANES))
                )
                span = slice(line * count, (line + 1) * count)
                left[turn, slot, span, :LANES] = hit * top
                left[turn, slot, span, LANES:] = hit * rest.astype(jnp.bfloat16)
            both = jnp.concatenate([spot, spot], axis=1)
            small[turn, slot * count : (slot + 1) * count] = dot(
                both, left[turn, slot], ((1,), (1,)), None
            )

    def settle(turn):
        top, rest = split(small[turn])
        named = jnp.where(same, jnp.broadcast_to(number[turn, 0:1], same.shape), -1.0)
        for tile in range(tiles_n):
            tiles[tile * count : (tile + 1) * count] = jnp.where(
                named == float(tile), 1.0, 0.0
            ).astype(jnp.bfloat16)
        acc[...] += dot(tiles[...], top, ((1,), (0,)), None) + dot(
            tiles[...], rest.astype(jnp.bfloat16), ((1,), (0,)), None
        )

    @pl.loop(0, devices // GROUP // 2)
    def _(pair):
        settle(1)
        squeeze(pair * 2, 0)
        settle(0)
        squeeze(pair * 2 + 1, 1)

    settle(1)
    most = LANES // count
    for first in range(0, cols_n, most):
        parts = range(first, min(first + most, cols_n))
        last = [acc[part * LANES : (part + 1) * LANES, LANES:] for part in parts]
        gap = LANES - len(last) * count
        if gap:
            last.append(jnp.zeros((LANES, gap), jnp.float32))
        last = jnp.concatenate(last, axis=1).T
        for part in parts:
            main = acc[part * LANES : (part + 1) * LANES, :LANES].T
            for line in range(COMPS):
                if line < most:
                    entry = main[line * count : (line + 1) * count]
                else:
                    entry = last[(part - first) * count : (part - first + 1) * count]
                start = line // 3 * (row_span * 3) + part * (count * 3) + line % 3
                spots = pl.ds(start, count, stride=3)
                out_ref[spots, :] = out_ref[spots, :] + entry


def local(rows_n, cols_n, coords, weights, values, rows, columns, owner, used, fill):
    count = coords.shape[-1]
    devices = rows_n * cols_n
    row_span = cols_n * count
    live_slots = rows.shape[2]
    slots = (live_slots + 15) // 16 * 16
    lots = GROUP * SLOTS
    dma = pltpu.SemaphoreType.DMA
    operands = (
        coords,
        weights,
        values.reshape(-1, 1, LANES),
        rows.reshape(-1, 1, LANES),
        columns.reshape(-1, 1, LANES),
        owner,
        used,
        fill,
    )
    out = pl.pallas_call(
        functools.partial(kernel, rows_n, cols_n),
        out_shape=jax.ShapeDtypeStruct((3 * row_span * 3, LANES), jnp.float32),
        in_specs=[
            pl.BlockSpec(memory_space=pltpu.SMEM if one is used else pltpu.HBM) for one in operands
        ],
        out_specs=pl.BlockSpec(memory_space=pltpu.VMEM),
        scratch_shapes=[
            pltpu.VMEM(coords.shape, jnp.float32),
            pltpu.VMEM(weights.shape, jnp.float32),
            pltpu.VMEM((slots * COMPS, LANES), jnp.float32),
            pltpu.VMEM((slots, LANES), jnp.int32),
            pltpu.VMEM((slots, LANES), jnp.int32),
            pltpu.VMEM(owner.shape, jnp.int32),
            pltpu.VMEM(fill.shape, jnp.int32),
            pltpu.VMEM((devices * RECORD, LANES), jnp.float32),
            pltpu.VMEM((devices * RECORD, LANES), jnp.float32),
            pltpu.VMEM((8, LANES), jnp.float32),
            pltpu.VMEM((rows_n, 8, LANES), jnp.float32),
            pltpu.VMEM((cols_n, 8, LANES), jnp.float32),
            pltpu.VMEM((cols_n, LANES, LANES), jnp.float32),
            pltpu.VMEM((2, lots, COMPS * count, 2 * LANES), jnp.bfloat16),
            pltpu.VMEM((2, lots * count, COMPS * count), jnp.float32),
            pltpu.VMEM((2, 8, lots * count), jnp.float32),
            pltpu.VMEM((devices * count, lots * count), jnp.bfloat16),
            pltpu.VMEM((devices * count, COMPS * count), jnp.float32),
            dma((len(operands) - 1,)),
            dma((devices,)),
            dma((devices,)),
            dma((rows_n,)),
            dma((rows_n,)),
            dma((cols_n,)),
            dma((cols_n,)),
        ],
        compiler_params=pltpu.CompilerParams(
            collective_id=0, has_side_effects=True, vmem_limit_bytes=40 * 1024 * 1024
        ),
    )(
        *(
            one if one is used else pltpu.with_memory_space_constraint(one, pltpu.HBM)
            for one in operands
        )
    )
    return out.reshape(1, 3, row_span, 3, 1, LANES)


def solution(mesh):
    placed = (
        P("col", "row", None, None, None),
        P("col", "row", None, None),
        P("row", "col", None, None, None),
        P("row", "col", None, None),
        P("row", "col", None, None),
        P("row", "col", None),
        P("row", "col"),
        P("row", "col", None),
    )
    return jax.shard_map(
        functools.partial(local, mesh.shape["row"], mesh.shape["col"]),
        mesh=mesh,
        in_specs=placed,
        out_specs=P("row", None, None, None, "col", None),
        check_vma=False,
    )
```

```python
import functools
import math

import jax
import jax.numpy as jnp
from jax import lax
from jax.experimental import pallas as pl
from jax.experimental.pallas import tpu as pltpu
from jax.sharding import PartitionSpec as P

MESH = pl.DeviceIdType.MESH
HIGH = lax.Precision.HIGHEST
CAP = 2
COMPS = 9
SLOTS = 2 * CAP
RECORD = SLOTS * (COMPS + 1)
LANES = 128
GROUP = 4
PAIR = 2

EPS_SQUARED = 0.01
KELVIN_A = 1.0 / (4.0 * math.pi)
KELVIN_B = KELVIN_A / 2.8
ISO_TERM = KELVIN_A - KELVIN_B
SOFT_TERM = KELVIN_A * 0.005
ANI_TERM = KELVIN_B


def dot(a, b, axes, precision=HIGH):
    return lax.dot_general(
        a, b, (axes, ((), ())), precision=precision, preferred_element_type=jnp.float32
    )


def split(value):
    top = value.astype(jnp.bfloat16)
    return top, value - top.astype(jnp.float32)


def halves(value):
    high, rest = split(value)
    return jnp.concatenate([high, rest.astype(jnp.bfloat16)], axis=0)


def iota(shape, axis):
    return lax.broadcasted_iota(jnp.int32, shape, axis)


def kernel(
    rows_n,
    cols_n,
    coords_hbm,
    weights_hbm,
    values_hbm,
    rows_hbm,
    columns_hbm,
    owner_hbm,
    used_ref,
    fill_hbm,
    out_ref,
    coords_ref,
    weights_ref,
    values_ref,
    rows_ref,
    columns_ref,
    owner_ref,
    fill_ref,
    send,
    recv,
    geo,
    geo_by_row,
    geo_by_col,
    row_geo,
    left,
    small,
    number,
    tiles,
    acc,
    load_sem,
    send_sem,
    recv_sem,
    row_send_sem,
    row_recv_sem,
    col_send_sem,
    col_recv_sem,
):
    my_row = lax.axis_index("row")
    my_col = lax.axis_index("col")
    devices = rows_n * cols_n
    me = my_row * cols_n + my_col
    points, count = coords_ref.shape[-2:]
    row_span = cols_n * count
    live_slots, _, width = rows_hbm.shape
    slots = rows_ref.shape[0]

    barrier = pltpu.get_barrier_semaphore()

    @pl.loop(1, devices)
    def _(k):
        other = (me + k) % devices
        pl.semaphore_signal(
            barrier,
            inc=1,
            device_id=(other // cols_n, other % cols_n),
            device_id_type=MESH,
        )

    lines_n = live_slots * COMPS
    loads = [
        pltpu.make_async_copy(source, target, load_sem.at[k])
        for k, (source, target) in enumerate(
            (
                (coords_hbm, coords_ref),
                (weights_hbm, weights_ref),
                (values_hbm.at[:, 0], values_ref.at[pl.ds(0, lines_n)]),
                (rows_hbm.at[:, 0], rows_ref.at[pl.ds(0, live_slots)]),
                (columns_hbm.at[:, 0], columns_ref.at[pl.ds(0, live_slots)]),
                (owner_hbm, owner_ref),
                (fill_hbm, fill_ref),
            )
        )
    ]
    edge = live_slots // 8 * 8
    rows_ref[edge:slots] = jnp.zeros((slots - edge, width), jnp.int32)
    columns_ref[edge:slots] = jnp.zeros((slots - edge, width), jnp.int32)
    edge = lines_n // 8 * 8
    values_ref[edge : slots * COMPS] = jnp.zeros((slots * COMPS - edge, width), jnp.float32)
    for load in loads:
        load.start()

    for load in loads[:2]:
        load.wait()
    spread = (iota((count, LANES), 1) % count == iota((count, LANES), 0)).astype(jnp.float32)
    at_point = iota((points, LANES), 1) // count == iota((points, LANES), 0)
    lines = []
    for comp in range(4):
        piece = coords_ref[0, 0, comp] if comp < 3 else weights_ref[0, 0]
        wide = dot(piece, spread, ((1,), (0,)))
        lines.append(jnp.sum(jnp.where(at_point, wide, 0.0), axis=0, keepdims=True))
    geo[...] = jnp.concatenate(lines + [jnp.zeros((4, LANES), jnp.float32)], axis=0)
    geo_by_col[0] = geo[...]
    geo_by_row[0] = geo[...]

    def row_copy(k):
        return pltpu.make_async_remote_copy(
            src_ref=geo,
            dst_ref=geo_by_row.at[k],
            send_sem=row_send_sem.at[k],
            recv_sem=row_recv_sem.at[k],
            device_id=((my_row + k) % rows_n, my_col),
            device_id_type=MESH,
        )

    def col_copy(k):
        return pltpu.make_async_remote_copy(
            src_ref=geo,
            dst_ref=geo_by_col.at[k],
            send_sem=col_send_sem.at[k],
            recv_sem=col_recv_sem.at[k],
            device_id=(my_row, (my_col + k) % cols_n),
            device_id_type=MESH,
        )

    for load in loads[2:]:
        load.wait()
    owner = jnp.concatenate([owner_ref[0], jnp.zeros((1, slots - live_slots), jnp.int32)], axis=1)
    fills = jnp.concatenate([fill_ref[0], jnp.zeros((1, slots - live_slots), jnp.int32)], axis=1)
    live = iota((1, slots), 1) < used_ref[0, 0]
    square = (slots, slots)
    diagonal = iota(square, 0) == iota(square, 1)
    fill = jnp.sum(jnp.where(diagonal, fills, 0), axis=1, keepdims=True)
    owner_down = jnp.sum(jnp.where(diagonal, owner, 0), axis=1, keepdims=True)
    row_position = rows_ref[...]
    column_position = columns_ref[...]
    row_group = row_position[:, 0:1] // count
    column_group = column_position[:, 0:1] // count
    mirror_down = column_group * cols_n + row_group
    mirror = jnp.sum(jnp.where(diagonal, mirror_down, 0), axis=0, keepdims=True)
    earlier = (iota(square, 0) < iota(square, 1)).astype(jnp.float32).astype(jnp.bfloat16)
    picks = []
    for target in (owner, mirror):
        named = ((target == iota((devices, slots), 0)) & live).astype(jnp.float32)
        rank = dot(named.astype(jnp.bfloat16), earlier, ((1,), (0,)), None)
        for place in range(CAP):
            picks.append(jnp.where(rank == float(place), named, 0.0))
    pick = jnp.concatenate(picks, axis=0).astype(jnp.bfloat16)
    pick = jnp.concatenate([pick, pick], axis=1)
    valid = iota((slots, width), 1) < fill
    row_inner = row_position % count
    column_inner = column_position % count
    forward = ((row_group * rows_n + column_group) * count + row_inner) * count + column_inner
    back_tile = owner_down % cols_n * rows_n + owner_down // cols_n
    backward = (back_tile * count + column_inner) * count + row_inner
    half = CAP * devices
    places = (
        dot(pick[:half], halves(forward.astype(jnp.float32)), ((1,), (0,)), None),
        dot(pick[half:], halves(backward.astype(jnp.float32)), ((1,), (0,)), None),
    )
    for slot in range(SLOTS):
        lot = places[slot // CAP][slot % CAP * devices : (slot % CAP + 1) * devices]
        send[pl.ds(SLOTS * COMPS + slot, devices, stride=RECORD), :] = lot
    for comp in range(COMPS):
        value = values_ref[pl.ds(comp, slots, stride=COMPS), :]
        sent = dot(pick, halves(jnp.where(valid, value, 0.0)), ((1,), (0,)), None)
        for slot in range(SLOTS):
            line = comp if slot < CAP else comp % 3 * 3 + comp // 3
            send[pl.ds(slot * COMPS + line, devices, stride=RECORD), :] = sent[
                slot * devices : (slot + 1) * devices
            ]

    pl.semaphore_wait(barrier, devices - 1)
    pl.loop(1, cols_n)(lambda k: col_copy(k).start())
    pl.loop(1, rows_n)(lambda k: row_copy(k).start())
    recv[0:RECORD, :] = send[pl.ds(pl.multiple_of(me * RECORD, 8), RECORD), :]

    def block_copy(k):
        other = me ^ k
        return pltpu.make_async_remote_copy(
            src_ref=send.at[pl.ds(pl.multiple_of(other * RECORD, 8), RECORD), :],
            dst_ref=recv.at[pl.ds(pl.multiple_of(k * RECORD, 8), RECORD), :],
            send_sem=send_sem.at[0],
            recv_sem=recv_sem.at[k // PAIR],
            device_id=(other // cols_n, other % cols_n),
            device_id_type=MESH,
        )

    pl.loop(1, devices)(lambda k: block_copy(k).start())

    pl.loop(1, cols_n)(lambda k: col_copy(k).wait())
    pl.loop(1, rows_n)(lambda k: row_copy(k).wait())

    lane = iota((8, LANES), 1)
    col_tiles = []
    for point in range(points):
        tile = jnp.zeros((8, LANES), jnp.float32)
        for part in range(rows_n):
            held = geo_by_row[(my_row - part + rows_n) % rows_n]
            shift = (part - point) * count % LANES
            if shift:
                held = pltpu.roll(held, shift, 1)
            tile = jnp.where(lane // count == part, held, tile)
        col_tiles.append(tile)
    for part in range(cols_n):
        held = geo_by_col[(my_col - part + cols_n) % cols_n]
        square_tile = jnp.concatenate(
            [held, jnp.zeros((LANES - 8, LANES), jnp.float32)], axis=0
        )
        row_geo[part] = square_tile.T

    @pl.loop(0, row_span // count)
    def _(part):
        def at_row_point(point, totals):
            start = pl.multiple_of(point * count, 8)
            here = [row_geo[part, pl.ds(start + first, 8), :] for first in range(0, count, 8)]
            spread = [
                [jnp.broadcast_to(one[:, comp : comp + 1], (8, LANES)) for comp in range(4)]
                for one in here
            ]
            totals = list(totals)
            for tile in col_tiles:
                bx, by, bz, bw = (tile[comp : comp + 1] for comp in range(4))
                for piece, (ax, ay, az, aw) in enumerate(spread):
                    xx, yy, xy, xz, yz, near, soft = totals[piece]
                    dx = ax - bx
                    dy = ay - by
                    dz = az - bz
                    inverse = lax.rsqrt(dx * dx + dy * dy + (dz * dz + EPS_SQUARED))
                    scaled = aw * bw * inverse
                    cubed = scaled * (inverse * inverse)
                    ex = cubed * dx
                    ey = cubed * dy
                    totals[piece] = (
                        xx + ex * dx,
                        yy + ey * dy,
                        xy + ex * dy,
                        xz + ex * dz,
                        yz + ey * dz,
                        near + scaled,
                        soft + cubed,
                    )
            return tuple(totals)

        zero = jnp.zeros((8, LANES), jnp.float32)
        totals = lax.fori_loop(
            0, points, at_row_point, ((zero,) * 7,) * (count // 8), unroll=True
        )
        for piece, (xx, yy, xy, xz, yz, near, soft) in enumerate(totals):
            zz = near - EPS_SQUARED * soft - xx - yy
            even = ISO_TERM * near + SOFT_TERM * soft
            xy, xz, yz = (ANI_TERM * term for term in (xy, xz, yz))
            xx, yy, zz = (ANI_TERM * term + even for term in (xx, yy, zz))
            for line, entry in enumerate((xx, xy, xz, xy, yy, yz, xz, yz, zz)):
                start = line // 3 * (row_span * 3) + part * (count * 3) + piece * 24 + line % 3
                out_ref[pl.ds(start, 8, stride=3), :] = entry

    lots = GROUP * SLOTS
    tiles_n = cols_n * rows_n
    acc[...] = jnp.zeros_like(acc)
    small[1] = jnp.zeros_like(small[1])
    number[1] = jnp.zeros_like(number[1])
    down = iota((count, LANES), 0).astype(jnp.float32)
    same = iota((count, lots * count), 1) % count == iota((count, lots * count), 0)
    mine_shape = (PAIR * SLOTS, PAIR * SLOTS * count)
    mine = iota(mine_shape, 0) == iota(mine_shape, 1) // count

    def arrived(first, records_n, sem):
        rows = pl.ds(pl.multiple_of(first * RECORD, 8), records_n * RECORD)
        other = me ^ 1
        return pltpu.make_async_remote_copy(
            src_ref=send.at[rows, :],
            dst_ref=recv.at[rows, :],
            send_sem=send_sem.at[0],
            recv_sem=sem,
            device_id=(other // cols_n, other % cols_n),
            device_id_type=MESH,
        )

    few = PAIR * SLOTS

    def squeeze(batch, turn):
        for part in range(GROUP // PAIR):
            first = batch * GROUP + part * PAIR
            sem = recv_sem.at[first // PAIR]
            if turn or part:
                arrived(first, PAIR, sem).wait_recv()
            else:
                pl.when(batch > 0)(lambda: arrived(first, PAIR, sem).wait_recv())
                pl.when(batch == 0)(lambda: arrived(1, PAIR - 1, sem).wait_recv())
            records = recv.at[pl.ds(pl.multiple_of(first * RECORD, 8), PAIR * RECORD), :]
            place = jnp.concatenate(
                [
                    records[inside * RECORD + SLOTS * COMPS : (inside + 1) * RECORD]
                    for inside in range(PAIR)
                ],
                axis=0,
            )
            whole = jnp.floor(place * (1.0 / (count * count)))
            inner = place - whole * (count * count)
            row_inner = jnp.floor(inner * (1.0 / count))
            column_inner = inner - row_inner * count
            lanes = slice(part * few * count, (part + 1) * few * count)
            number[turn, :, lanes] = jnp.broadcast_to(
                jnp.sum(jnp.where(mine, whole[:, 0:1], 0.0), axis=0, keepdims=True),
                (8, few * count),
            )
            for slot in range(few):
                line = slot // SLOTS * RECORD + slot % SLOTS * COMPS
                at = part * few + slot
                hit = jnp.where(row_inner[slot : slot + 1] == down, 1.0, 0.0).astype(jnp.bfloat16)
                spot = jnp.where(column_inner[slot : slot + 1] == down, 1.0, 0.0).astype(
                    jnp.bfloat16
                )
                for comp in range(COMPS):
                    top, rest = split(
                        jnp.broadcast_to(records[line + comp : line + comp + 1], (count, LANES))
                    )
                    span = slice(comp * count, (comp + 1) * count)
                    left[turn, at, span, :LANES] = hit * top
                    left[turn, at, span, LANES:] = hit * rest.astype(jnp.bfloat16)
                both = jnp.concatenate([spot, spot], axis=1)
                small[turn, at * count : (at + 1) * count] = dot(
                    both, left[turn, at], ((1,), (1,)), None
                )

    def settle(turn):
        top, rest = split(small[turn])
        named = jnp.where(same, jnp.broadcast_to(number[turn, 0:1], same.shape), -1.0)
        for tile in range(tiles_n):
            tiles[tile * count : (tile + 1) * count] = jnp.where(
                named == float(tile), 1.0, 0.0
            ).astype(jnp.bfloat16)
        acc[...] += dot(tiles[...], top, ((1,), (0,)), None) + dot(
            tiles[...], rest.astype(jnp.bfloat16), ((1,), (0,)), None
        )

    @pl.loop(0, devices // GROUP // 2)
    def _(pair):
        settle(1)
        squeeze(pair * 2, 0)
        settle(0)
        squeeze(pair * 2 + 1, 1)

    arrived(1, devices - 1, recv_sem.at[0]).wait_send()
    settle(1)
    most = LANES // count
    for first in range(0, cols_n, most):
        parts = range(first, min(first + most, cols_n))
        last = [acc[part * LANES : (part + 1) * LANES, LANES:] for part in parts]
        gap = LANES - len(last) * count
        if gap:
            last.append(jnp.zeros((LANES, gap), jnp.float32))
        last = jnp.concatenate(last, axis=1).T
        for part in parts:
            main = acc[part * LANES : (part + 1) * LANES, :LANES].T
            for line in range(COMPS):
                if line < most:
                    entry = main[line * count : (line + 1) * count]
                else:
                    entry = last[(part - first) * count : (part - first + 1) * count]
                start = line // 3 * (row_span * 3) + part * (count * 3) + line % 3
                spots = pl.ds(start, count, stride=3)
                out_ref[spots, :] = out_ref[spots, :] + entry


def local(rows_n, cols_n, coords, weights, values, rows, columns, owner, used, fill):
    count = coords.shape[-1]
    devices = rows_n * cols_n
    row_span = cols_n * count
    live_slots = rows.shape[2]
    slots = (live_slots + 15) // 16 * 16
    lots = GROUP * SLOTS
    dma = pltpu.SemaphoreType.DMA
    operands = (
        coords,
        weights,
        values.reshape(-1, 1, LANES),
        rows.reshape(-1, 1, LANES),
        columns.reshape(-1, 1, LANES),
        owner,
        used,
        fill,
    )
    out = pl.pallas_call(
        functools.partial(kernel, rows_n, cols_n),
        out_shape=jax.ShapeDtypeStruct((3 * row_span * 3, LANES), jnp.float32),
        in_specs=[
            pl.BlockSpec(memory_space=pltpu.SMEM if one is used else pltpu.HBM) for one in operands
        ],
        out_specs=pl.BlockSpec(memory_space=pltpu.VMEM),
        scratch_shapes=[
            pltpu.VMEM(coords.shape, jnp.float32),
            pltpu.VMEM(weights.shape, jnp.float32),
            pltpu.VMEM((slots * COMPS, LANES), jnp.float32),
            pltpu.VMEM((slots, LANES), jnp.int32),
            pltpu.VMEM((slots, LANES), jnp.int32),
            pltpu.VMEM(owner.shape, jnp.int32),
            pltpu.VMEM(fill.shape, jnp.int32),
            pltpu.VMEM((devices * RECORD, LANES), jnp.float32),
            pltpu.VMEM((devices * RECORD, LANES), jnp.float32),
            pltpu.VMEM((8, LANES), jnp.float32),
            pltpu.VMEM((rows_n, 8, LANES), jnp.float32),
            pltpu.VMEM((cols_n, 8, LANES), jnp.float32),
            pltpu.VMEM((cols_n, LANES, LANES), jnp.float32),
            pltpu.VMEM((2, lots, COMPS * count, 2 * LANES), jnp.bfloat16),
            pltpu.VMEM((2, lots * count, COMPS * count), jnp.float32),
            pltpu.VMEM((2, 8, lots * count), jnp.float32),
            pltpu.VMEM((devices * count, lots * count), jnp.bfloat16),
            pltpu.VMEM((devices * count, COMPS * count), jnp.float32),
            dma((len(operands) - 1,)),
            dma((1,)),
            dma((devices // PAIR,)),
            dma((rows_n,)),
            dma((rows_n,)),
            dma((cols_n,)),
            dma((cols_n,)),
        ],
        compiler_params=pltpu.CompilerParams(
            collective_id=0, has_side_effects=True, vmem_limit_bytes=40 * 1024 * 1024
        ),
    )(
        *(
            one if one is used else pltpu.with_memory_space_constraint(one, pltpu.HBM)
            for one in operands
        )
    )
    return out.reshape(1, 3, row_span, 3, 1, LANES)


def solution(mesh):
    placed = (
        P("col", "row", None, None, None),
        P("col", "row", None, None),
        P("row", "col", None, None, None),
        P("row", "col", None, None),
        P("row", "col", None, None),
        P("row", "col", None),
        P("row", "col"),
        P("row", "col", None),
    )
    return jax.shard_map(
        functools.partial(local, mesh.shape["row"], mesh.shape["col"]),
        mesh=mesh,
        in_specs=placed,
        out_specs=P("row", None, None, None, "col", None),
        check_vma=False,
    )
```

```python
import functools
import math

import jax
import jax.numpy as jnp
from jax import lax
from jax.experimental import pallas as pl
from jax.experimental.pallas import tpu as pltpu
from jax.sharding import PartitionSpec as P

MESH = pl.DeviceIdType.MESH
HIGH = lax.Precision.HIGHEST
CAP = 2
COMPS = 9
SLOTS = 2 * CAP
RECORD = SLOTS * (COMPS + 1)
LANES = 128
GROUP = 4
PAIR = 2

EPS_SQUARED = 0.01
KELVIN_A = 1.0 / (4.0 * math.pi)
KELVIN_B = KELVIN_A / 2.8
ISO_TERM = KELVIN_A - KELVIN_B
SOFT_TERM = KELVIN_A * 0.005
ANI_TERM = KELVIN_B


def dot(a, b, axes, precision=HIGH):
    return lax.dot_general(
        a, b, (axes, ((), ())), precision=precision, preferred_element_type=jnp.float32
    )


def split(value):
    top = value.astype(jnp.bfloat16)
    return top, value - top.astype(jnp.float32)


def halves(value):
    high, rest = split(value)
    return jnp.concatenate([high, rest.astype(jnp.bfloat16)], axis=0)


def iota(shape, axis):
    return lax.broadcasted_iota(jnp.int32, shape, axis)


def kernel(
    rows_n,
    cols_n,
    coords_hbm,
    weights_hbm,
    values_hbm,
    rows_hbm,
    columns_hbm,
    owner_hbm,
    used_ref,
    fill_hbm,
    out_ref,
    coords_ref,
    weights_ref,
    values_ref,
    rows_ref,
    columns_ref,
    owner_ref,
    fill_ref,
    send,
    recv,
    geo,
    geo_by_row,
    geo_by_col,
    row_geo,
    left,
    small,
    number,
    tiles,
    acc,
    load_sem,
    send_sem,
    recv_sem,
    row_send_sem,
    row_recv_sem,
    col_send_sem,
    col_recv_sem,
):
    my_row = lax.axis_index("row")
    my_col = lax.axis_index("col")
    devices = rows_n * cols_n
    me = my_row * cols_n + my_col
    points, count = coords_ref.shape[-2:]
    row_span = cols_n * count
    live_slots, _, width = rows_hbm.shape
    slots = rows_ref.shape[0]

    barrier = pltpu.get_barrier_semaphore()

    @pl.loop(1, devices, unroll=True)
    def _(k):
        other = me ^ (devices - k)
        pl.semaphore_signal(
            barrier,
            inc=1,
            device_id=(other // cols_n, other % cols_n),
            device_id_type=MESH,
        )

    lines_n = live_slots * COMPS
    loads = [
        pltpu.make_async_copy(source, target, load_sem.at[k])
        for k, (source, target) in enumerate(
            (
                (coords_hbm, coords_ref),
                (weights_hbm, weights_ref),
                (values_hbm.at[:, 0], values_ref.at[pl.ds(0, lines_n)]),
                (rows_hbm.at[:, 0], rows_ref.at[pl.ds(0, live_slots)]),
                (columns_hbm.at[:, 0], columns_ref.at[pl.ds(0, live_slots)]),
                (owner_hbm, owner_ref),
                (fill_hbm, fill_ref),
            )
        )
    ]
    edge = live_slots // 8 * 8
    rows_ref[edge:slots] = jnp.zeros((slots - edge, width), jnp.int32)
    columns_ref[edge:slots] = jnp.zeros((slots - edge, width), jnp.int32)
    edge = lines_n // 8 * 8
    values_ref[edge : slots * COMPS] = jnp.zeros((slots * COMPS - edge, width), jnp.float32)
    for load in loads:
        load.start()

    for load in loads[:2]:
        load.wait()
    spread = (iota((count, LANES), 1) % count == iota((count, LANES), 0)).astype(jnp.float32)
    at_point = iota((points, LANES), 1) // count == iota((points, LANES), 0)
    lines = []
    for comp in range(4):
        piece = coords_ref[0, 0, comp] if comp < 3 else weights_ref[0, 0]
        wide = dot(piece, spread, ((1,), (0,)))
        lines.append(jnp.sum(jnp.where(at_point, wide, 0.0), axis=0, keepdims=True))
    geo[...] = jnp.concatenate(lines + [jnp.zeros((4, LANES), jnp.float32)], axis=0)
    geo_by_col[0] = geo[...]
    geo_by_row[0] = geo[...]

    def row_copy(k):
        return pltpu.make_async_remote_copy(
            src_ref=geo,
            dst_ref=geo_by_row.at[k],
            send_sem=row_send_sem.at[k],
            recv_sem=row_recv_sem.at[k],
            device_id=((my_row + k) % rows_n, my_col),
            device_id_type=MESH,
        )

    def col_copy(k):
        return pltpu.make_async_remote_copy(
            src_ref=geo,
            dst_ref=geo_by_col.at[k],
            send_sem=col_send_sem.at[k],
            recv_sem=col_recv_sem.at[k],
            device_id=(my_row, (my_col + k) % cols_n),
            device_id_type=MESH,
        )

    for load in loads[2:]:
        load.wait()
    owner = jnp.concatenate([owner_ref[0], jnp.zeros((1, slots - live_slots), jnp.int32)], axis=1)
    fills = jnp.concatenate([fill_ref[0], jnp.zeros((1, slots - live_slots), jnp.int32)], axis=1)
    live = iota((1, slots), 1) < used_ref[0, 0]
    square = (slots, slots)
    diagonal = iota(square, 0) == iota(square, 1)
    fill = jnp.sum(jnp.where(diagonal, fills, 0), axis=1, keepdims=True)
    owner_down = jnp.sum(jnp.where(diagonal, owner, 0), axis=1, keepdims=True)
    row_position = rows_ref[...]
    column_position = columns_ref[...]
    row_group = row_position[:, 0:1] // count
    column_group = column_position[:, 0:1] // count
    mirror_down = column_group * cols_n + row_group
    mirror = jnp.sum(jnp.where(diagonal, mirror_down, 0), axis=0, keepdims=True)
    earlier = (iota(square, 0) < iota(square, 1)).astype(jnp.float32).astype(jnp.bfloat16)
    picks = []
    for target in (owner, mirror):
        named = ((target == iota((devices, slots), 0)) & live).astype(jnp.float32)
        rank = dot(named.astype(jnp.bfloat16), earlier, ((1,), (0,)), None)
        for place in range(CAP):
            picks.append(jnp.where(rank == float(place), named, 0.0))
    pick = jnp.concatenate(picks, axis=0).astype(jnp.bfloat16)
    pick = jnp.concatenate([pick, pick], axis=1)
    valid = iota((slots, width), 1) < fill
    row_inner = row_position % count
    column_inner = column_position % count
    forward = ((row_group * rows_n + column_group) * count + row_inner) * count + column_inner
    back_tile = owner_down % cols_n * rows_n + owner_down // cols_n
    backward = (back_tile * count + column_inner) * count + row_inner
    half = CAP * devices
    places = (
        dot(pick[:half], halves(forward.astype(jnp.float32)), ((1,), (0,)), None),
        dot(pick[half:], halves(backward.astype(jnp.float32)), ((1,), (0,)), None),
    )
    for slot in range(SLOTS):
        lot = places[slot // CAP][slot % CAP * devices : (slot % CAP + 1) * devices]
        send[pl.ds(SLOTS * COMPS + slot, devices, stride=RECORD), :] = lot
    for comp in range(COMPS):
        value = values_ref[pl.ds(comp, slots, stride=COMPS), :]
        sent = dot(pick, halves(jnp.where(valid, value, 0.0)), ((1,), (0,)), None)
        for slot in range(SLOTS):
            line = comp if slot < CAP else comp % 3 * 3 + comp // 3
            send[pl.ds(slot * COMPS + line, devices, stride=RECORD), :] = sent[
                slot * devices : (slot + 1) * devices
            ]

    pl.semaphore_wait(barrier, devices - 1)
    for k in range(1, cols_n):
        col_copy(k).start()
    for k in range(1, rows_n):
        row_copy(k).start()
    recv[0:RECORD, :] = send[pl.ds(pl.multiple_of(me * RECORD, 8), RECORD), :]

    def block_copy(k):
        other = me ^ k
        return pltpu.make_async_remote_copy(
            src_ref=send.at[pl.ds(pl.multiple_of(other * RECORD, 8), RECORD), :],
            dst_ref=recv.at[pl.ds(pl.multiple_of(k * RECORD, 8), RECORD), :],
            send_sem=send_sem.at[0],
            recv_sem=recv_sem.at[k // PAIR],
            device_id=(other // cols_n, other % cols_n),
            device_id_type=MESH,
        )

    for k in range(1, devices):
        block_copy(k).start()

    pl.loop(1, cols_n)(lambda k: col_copy(k).wait())
    pl.loop(1, rows_n)(lambda k: row_copy(k).wait())

    lane = iota((8, LANES), 1)
    col_tiles = []
    for point in range(points):
        tile = jnp.zeros((8, LANES), jnp.float32)
        for part in range(rows_n):
            held = geo_by_row[(my_row - part + rows_n) % rows_n]
            shift = (part - point) * count % LANES
            if shift:
                held = pltpu.roll(held, shift, 1)
            tile = jnp.where(lane // count == part, held, tile)
        col_tiles.append(tile)
    for part in range(cols_n):
        held = geo_by_col[(my_col - part + cols_n) % cols_n]
        square_tile = jnp.concatenate(
            [held, jnp.zeros((LANES - 8, LANES), jnp.float32)], axis=0
        )
        row_geo[part] = square_tile.T

    @pl.loop(0, row_span // count)
    def _(part):
        def at_row_point(point, totals):
            start = pl.multiple_of(point * count, 8)
            here = [row_geo[part, pl.ds(start + first, 8), :] for first in range(0, count, 8)]
            spread = [
                [jnp.broadcast_to(one[:, comp : comp + 1], (8, LANES)) for comp in range(4)]
                for one in here
            ]
            totals = list(totals)
            for tile in col_tiles:
                bx, by, bz, bw = (tile[comp : comp + 1] for comp in range(4))
                for piece, (ax, ay, az, aw) in enumerate(spread):
                    xx, yy, xy, xz, yz, near, soft = totals[piece]
                    dx = ax - bx
                    dy = ay - by
                    dz = az - bz
                    inverse = lax.rsqrt(dx * dx + dy * dy + (dz * dz + EPS_SQUARED))
                    scaled = aw * bw * inverse
                    cubed = scaled * (inverse * inverse)
                    ex = cubed * dx
                    ey = cubed * dy
                    totals[piece] = (
                        xx + ex * dx,
                        yy + ey * dy,
                        xy + ex * dy,
                        xz + ex * dz,
                        yz + ey * dz,
                        near + scaled,
                        soft + cubed,
                    )
            return tuple(totals)

        zero = jnp.zeros((8, LANES), jnp.float32)
        totals = lax.fori_loop(
            0, points, at_row_point, ((zero,) * 7,) * (count // 8), unroll=True
        )
        for piece, (xx, yy, xy, xz, yz, near, soft) in enumerate(totals):
            zz = near - EPS_SQUARED * soft - xx - yy
            even = ISO_TERM * near + SOFT_TERM * soft
            xy, xz, yz = (ANI_TERM * term for term in (xy, xz, yz))
            xx, yy, zz = (ANI_TERM * term + even for term in (xx, yy, zz))
            for line, entry in enumerate((xx, xy, xz, xy, yy, yz, xz, yz, zz)):
                start = line // 3 * (row_span * 3) + part * (count * 3) + piece * 24 + line % 3
                out_ref[pl.ds(start, 8, stride=3), :] = entry

    lots = GROUP * SLOTS
    tiles_n = cols_n * rows_n
    acc[...] = jnp.zeros_like(acc)
    small[1] = jnp.zeros_like(small[1])
    number[1] = jnp.zeros_like(number[1])
    down = iota((count, LANES), 0).astype(jnp.float32)
    same = iota((count, lots * count), 1) % count == iota((count, lots * count), 0)
    mine_shape = (PAIR * SLOTS, PAIR * SLOTS * count)
    mine = iota(mine_shape, 0) == iota(mine_shape, 1) // count

    def arrived(first, records_n, sem):
        rows = pl.ds(pl.multiple_of(first * RECORD, 8), records_n * RECORD)
        other = me ^ 1
        return pltpu.make_async_remote_copy(
            src_ref=send.at[rows, :],
            dst_ref=recv.at[rows, :],
            send_sem=send_sem.at[0],
            recv_sem=sem,
            device_id=(other // cols_n, other % cols_n),
            device_id_type=MESH,
        )

    few = PAIR * SLOTS

    def squeeze(batch, turn):
        for part in range(GROUP // PAIR):
            first = batch * GROUP + part * PAIR
            sem = recv_sem.at[first // PAIR]
            if turn or part:
                arrived(first, PAIR, sem).wait_recv()
            else:
                pl.when(batch > 0)(lambda: arrived(first, PAIR, sem).wait_recv())
                pl.when(batch == 0)(lambda: arrived(1, PAIR - 1, sem).wait_recv())
            records = recv.at[pl.ds(pl.multiple_of(first * RECORD, 8), PAIR * RECORD), :]
            place = jnp.concatenate(
                [
                    records[inside * RECORD + SLOTS * COMPS : (inside + 1) * RECORD]
                    for inside in range(PAIR)
                ],
                axis=0,
            )
            whole = jnp.floor(place * (1.0 / (count * count)))
            inner = place - whole * (count * count)
            row_inner = jnp.floor(inner * (1.0 / count))
            column_inner = inner - row_inner * count
            lanes = slice(part * few * count, (part + 1) * few * count)
            number[turn, :, lanes] = jnp.broadcast_to(
                jnp.sum(jnp.where(mine, whole[:, 0:1], 0.0), axis=0, keepdims=True),
                (8, few * count),
            )
            for slot in range(few):
                line = slot // SLOTS * RECORD + slot % SLOTS * COMPS
                at = part * few + slot
                hit = jnp.where(row_inner[slot : slot + 1] == down, 1.0, 0.0).astype(jnp.bfloat16)
                spot = jnp.where(column_inner[slot : slot + 1] == down, 1.0, 0.0).astype(
                    jnp.bfloat16
                )
                for comp in range(COMPS):
                    top, rest = split(
                        jnp.broadcast_to(records[line + comp : line + comp + 1], (count, LANES))
                    )
                    span = slice(comp * count, (comp + 1) * count)
                    left[turn, at, span, :LANES] = hit * top
                    left[turn, at, span, LANES:] = hit * rest.astype(jnp.bfloat16)
                both = jnp.concatenate([spot, spot], axis=1)
                small[turn, at * count : (at + 1) * count] = dot(
                    both, left[turn, at], ((1,), (1,)), None
                )

    def settle(turn):
        top, rest = split(small[turn])
        named = jnp.where(same, jnp.broadcast_to(number[turn, 0:1], same.shape), -1.0)
        for tile in range(tiles_n):
            tiles[tile * count : (tile + 1) * count] = jnp.where(
                named == float(tile), 1.0, 0.0
            ).astype(jnp.bfloat16)
        acc[...] += dot(tiles[...], top, ((1,), (0,)), None) + dot(
            tiles[...], rest.astype(jnp.bfloat16), ((1,), (0,)), None
        )

    @pl.loop(0, devices // GROUP // 2)
    def _(pair):
        settle(1)
        squeeze(pair * 2, 0)
        settle(0)
        squeeze(pair * 2 + 1, 1)

    arrived(1, devices - 1, recv_sem.at[0]).wait_send()
    settle(1)
    most = LANES // count
    for first in range(0, cols_n, most):
        parts = range(first, min(first + most, cols_n))
        last = [acc[part * LANES : (part + 1) * LANES, LANES:] for part in parts]
        gap = LANES - len(last) * count
        if gap:
            last.append(jnp.zeros((LANES, gap), jnp.float32))
        last = jnp.concatenate(last, axis=1).T
        for part in parts:
            main = acc[part * LANES : (part + 1) * LANES, :LANES].T
            for line in range(COMPS):
                if line < most:
                    entry = main[line * count : (line + 1) * count]
                else:
                    entry = last[(part - first) * count : (part - first + 1) * count]
                start = line // 3 * (row_span * 3) + part * (count * 3) + line % 3
                spots = pl.ds(start, count, stride=3)
                out_ref[spots, :] = out_ref[spots, :] + entry


def local(rows_n, cols_n, coords, weights, values, rows, columns, owner, used, fill):
    count = coords.shape[-1]
    devices = rows_n * cols_n
    row_span = cols_n * count
    live_slots = rows.shape[2]
    slots = (live_slots + 15) // 16 * 16
    lots = GROUP * SLOTS
    dma = pltpu.SemaphoreType.DMA
    operands = (
        coords,
        weights,
        values.reshape(-1, 1, LANES),
        rows.reshape(-1, 1, LANES),
        columns.reshape(-1, 1, LANES),
        owner,
        used,
        fill,
    )
    out = pl.pallas_call(
        functools.partial(kernel, rows_n, cols_n),
        out_shape=jax.ShapeDtypeStruct((3 * row_span * 3, LANES), jnp.float32),
        in_specs=[
            pl.BlockSpec(memory_space=pltpu.SMEM if one is used else pltpu.HBM) for one in operands
        ],
        out_specs=pl.BlockSpec(memory_space=pltpu.VMEM),
        scratch_shapes=[
            pltpu.VMEM(coords.shape, jnp.float32),
            pltpu.VMEM(weights.shape, jnp.float32),
            pltpu.VMEM((slots * COMPS, LANES), jnp.float32),
            pltpu.VMEM((slots, LANES), jnp.int32),
            pltpu.VMEM((slots, LANES), jnp.int32),
            pltpu.VMEM(owner.shape, jnp.int32),
            pltpu.VMEM(fill.shape, jnp.int32),
            pltpu.VMEM((devices * RECORD, LANES), jnp.float32),
            pltpu.VMEM((devices * RECORD, LANES), jnp.float32),
            pltpu.VMEM((8, LANES), jnp.float32),
            pltpu.VMEM((rows_n, 8, LANES), jnp.float32),
            pltpu.VMEM((cols_n, 8, LANES), jnp.float32),
            pltpu.VMEM((cols_n, LANES, LANES), jnp.float32),
            pltpu.VMEM((2, lots, COMPS * count, 2 * LANES), jnp.bfloat16),
            pltpu.VMEM((2, lots * count, COMPS * count), jnp.float32),
            pltpu.VMEM((2, 8, lots * count), jnp.float32),
            pltpu.VMEM((devices * count, lots * count), jnp.bfloat16),
            pltpu.VMEM((devices * count, COMPS * count), jnp.float32),
            dma((len(operands) - 1,)),
            dma((1,)),
            dma((devices // PAIR,)),
            dma((rows_n,)),
            dma((rows_n,)),
            dma((cols_n,)),
            dma((cols_n,)),
        ],
        compiler_params=pltpu.CompilerParams(
            collective_id=0, has_side_effects=True, vmem_limit_bytes=40 * 1024 * 1024
        ),
    )(
        *(
            one if one is used else pltpu.with_memory_space_constraint(one, pltpu.HBM)
            for one in operands
        )
    )
    return out.reshape(1, 3, row_span, 3, 1, LANES)


def solution(mesh):
    placed = (
        P("col", "row", None, None, None),
        P("col", "row", None, None),
        P("row", "col", None, None, None),
        P("row", "col", None, None),
        P("row", "col", None, None),
        P("row", "col", None),
        P("row", "col"),
        P("row", "col", None),
    )
    return jax.shard_map(
        functools.partial(local, mesh.shape["row"], mesh.shape["col"]),
        mesh=mesh,
        in_specs=placed,
        out_specs=P("row", None, None, None, "col", None),
        check_vma=False,
    )
```

```python
import functools
import math

import jax
import jax.numpy as jnp
from jax import lax
from jax.experimental import pallas as pl
from jax.experimental.pallas import tpu as pltpu
from jax.sharding import PartitionSpec as P

MESH = pl.DeviceIdType.MESH
HIGH = lax.Precision.HIGHEST
CAP = 2
COMPS = 9
SLOTS = 2 * CAP
RECORD = SLOTS * (COMPS + 1)
LANES = 128
GROUP = 4
PAIR = 2

EPS_SQUARED = 0.01
KELVIN_A = 1.0 / (4.0 * math.pi)
KELVIN_B = KELVIN_A / 2.8
ISO_TERM = KELVIN_A - KELVIN_B
SOFT_TERM = KELVIN_A * 0.005
ANI_TERM = KELVIN_B


def dot(a, b, axes, precision=HIGH):
    return lax.dot_general(
        a, b, (axes, ((), ())), precision=precision, preferred_element_type=jnp.float32
    )


def split(value):
    top = value.astype(jnp.bfloat16)
    return top, value - top.astype(jnp.float32)


def halves(value):
    high, rest = split(value)
    return jnp.concatenate([high, rest.astype(jnp.bfloat16)], axis=0)


def iota(shape, axis):
    return lax.broadcasted_iota(jnp.int32, shape, axis)


def kernel(
    rows_n,
    cols_n,
    coords_hbm,
    weights_hbm,
    values_hbm,
    rows_hbm,
    columns_hbm,
    owner_hbm,
    used_ref,
    fill_hbm,
    out_ref,
    coords_ref,
    weights_ref,
    values_ref,
    rows_ref,
    columns_ref,
    owner_ref,
    fill_ref,
    send,
    recv,
    geo,
    geo_by_row,
    geo_by_col,
    row_geo,
    left,
    small,
    number,
    tiles,
    acc,
    load_sem,
    send_sem,
    recv_sem,
    row_send_sem,
    row_recv_sem,
    col_send_sem,
    col_recv_sem,
):
    my_row = lax.axis_index("row")
    my_col = lax.axis_index("col")
    devices = rows_n * cols_n
    me = my_row * cols_n + my_col
    points, count = coords_ref.shape[-2:]
    row_span = cols_n * count
    live_slots, _, width = rows_hbm.shape
    slots = rows_ref.shape[0]

    barrier = pltpu.get_barrier_semaphore()

    @pl.loop(1, devices, unroll=True)
    def _(k):
        other = me ^ (devices - k)
        pl.semaphore_signal(
            barrier,
            inc=1,
            device_id=(other // cols_n, other % cols_n),
            device_id_type=MESH,
        )

    lines_n = live_slots * COMPS
    loads = [
        pltpu.make_async_copy(source, target, load_sem.at[k])
        for k, (source, target) in enumerate(
            (
                (coords_hbm, coords_ref),
                (weights_hbm, weights_ref),
                (values_hbm.at[:, 0], values_ref.at[pl.ds(0, lines_n)]),
                (rows_hbm.at[:, 0], rows_ref.at[pl.ds(0, live_slots)]),
                (columns_hbm.at[:, 0], columns_ref.at[pl.ds(0, live_slots)]),
                (owner_hbm, owner_ref),
                (fill_hbm, fill_ref),
            )
        )
    ]
    edge = live_slots // 8 * 8
    rows_ref[edge:slots] = jnp.zeros((slots - edge, width), jnp.int32)
    columns_ref[edge:slots] = jnp.zeros((slots - edge, width), jnp.int32)
    edge = lines_n // 8 * 8
    values_ref[edge : slots * COMPS] = jnp.zeros((slots * COMPS - edge, width), jnp.float32)
    for load in loads:
        load.start()

    for load in loads[:2]:
        load.wait()
    spread = (iota((count, LANES), 1) % count == iota((count, LANES), 0)).astype(jnp.float32)
    at_point = iota((points, LANES), 1) // count == iota((points, LANES), 0)
    lines = []
    for comp in range(4):
        piece = coords_ref[0, 0, comp] if comp < 3 else weights_ref[0, 0]
        wide = dot(piece, spread, ((1,), (0,)))
        lines.append(jnp.sum(jnp.where(at_point, wide, 0.0), axis=0, keepdims=True))
    geo[...] = jnp.concatenate(lines + [jnp.zeros((4, LANES), jnp.float32)], axis=0)
    geo_by_col[0] = geo[...]
    geo_by_row[0] = geo[...]

    def row_copy(k):
        return pltpu.make_async_remote_copy(
            src_ref=geo,
            dst_ref=geo_by_row.at[k],
            send_sem=row_send_sem.at[k],
            recv_sem=row_recv_sem.at[k],
            device_id=((my_row + k) % rows_n, my_col),
            device_id_type=MESH,
        )

    def col_copy(k):
        return pltpu.make_async_remote_copy(
            src_ref=geo,
            dst_ref=geo_by_col.at[k],
            send_sem=col_send_sem.at[k],
            recv_sem=col_recv_sem.at[k],
            device_id=(my_row, (my_col + k) % cols_n),
            device_id_type=MESH,
        )

    for load in loads[2:]:
        load.wait()
    owner = jnp.concatenate([owner_ref[0], jnp.zeros((1, slots - live_slots), jnp.int32)], axis=1)
    fills = jnp.concatenate([fill_ref[0], jnp.zeros((1, slots - live_slots), jnp.int32)], axis=1)
    live = iota((1, slots), 1) < used_ref[0, 0]
    square = (slots, slots)
    diagonal = iota(square, 0) == iota(square, 1)
    fill = jnp.sum(jnp.where(diagonal, fills, 0), axis=1, keepdims=True)
    owner_down = jnp.sum(jnp.where(diagonal, owner, 0), axis=1, keepdims=True)
    row_position = rows_ref[...]
    column_position = columns_ref[...]
    row_group = row_position[:, 0:1] // count
    column_group = column_position[:, 0:1] // count
    mirror_down = column_group * cols_n + row_group
    mirror = jnp.sum(jnp.where(diagonal, mirror_down, 0), axis=0, keepdims=True)
    earlier = (iota(square, 0) < iota(square, 1)).astype(jnp.float32).astype(jnp.bfloat16)
    picks = []
    for target in (owner, mirror):
        named = ((target == iota((devices, slots), 0)) & live).astype(jnp.float32)
        rank = dot(named.astype(jnp.bfloat16), earlier, ((1,), (0,)), None)
        for place in range(CAP):
            picks.append(jnp.where(rank == float(place), named, 0.0))
    pick = jnp.concatenate(picks, axis=0).astype(jnp.bfloat16)
    pick = jnp.concatenate([pick, pick], axis=1)
    valid = iota((slots, width), 1) < fill
    row_inner = row_position % count
    column_inner = column_position % count
    forward = ((row_group * rows_n + column_group) * count + row_inner) * count + column_inner
    back_tile = owner_down % cols_n * rows_n + owner_down // cols_n
    backward = (back_tile * count + column_inner) * count + row_inner
    half = CAP * devices
    places = (
        dot(pick[:half], halves(forward.astype(jnp.float32)), ((1,), (0,)), None),
        dot(pick[half:], halves(backward.astype(jnp.float32)), ((1,), (0,)), None),
    )
    for slot in range(SLOTS):
        lot = places[slot // CAP][slot % CAP * devices : (slot % CAP + 1) * devices]
        send[pl.ds(SLOTS * COMPS + slot, devices, stride=RECORD), :] = lot
    for comp in range(COMPS):
        value = values_ref[pl.ds(comp, slots, stride=COMPS), :]
        sent = dot(pick, halves(jnp.where(valid, value, 0.0)), ((1,), (0,)), None)
        for slot in range(SLOTS):
            line = comp if slot < CAP else comp % 3 * 3 + comp // 3
            send[pl.ds(slot * COMPS + line, devices, stride=RECORD), :] = sent[
                slot * devices : (slot + 1) * devices
            ]

    pl.semaphore_wait(barrier, devices - 1)
    for k in range(1, cols_n):
        col_copy(k).start()
    for k in range(1, rows_n):
        row_copy(k).start()
    recv[0:RECORD, :] = send[pl.ds(pl.multiple_of(me * RECORD, 8), RECORD), :]

    def block_copy(k):
        other = me ^ k
        return pltpu.make_async_remote_copy(
            src_ref=send.at[pl.ds(pl.multiple_of(other * RECORD, 8), RECORD), :],
            dst_ref=recv.at[pl.ds(pl.multiple_of(k * RECORD, 8), RECORD), :],
            send_sem=send_sem.at[0],
            recv_sem=recv_sem.at[k // PAIR],
            device_id=(other // cols_n, other % cols_n),
            device_id_type=MESH,
        )

    for k in range(1, devices):
        block_copy(k if k < 2 else k ^ 1).start()

    def kelvin():
        pl.loop(1, cols_n)(lambda k: col_copy(k).wait())
        pl.loop(1, rows_n)(lambda k: row_copy(k).wait())

        lane = iota((8, LANES), 1)
        col_tiles = []
        for point in range(points):
            tile = jnp.zeros((8, LANES), jnp.float32)
            for part in range(rows_n):
                held = geo_by_row[(my_row - part + rows_n) % rows_n]
                shift = (part - point) * count % LANES
                if shift:
                    held = pltpu.roll(held, shift, 1)
                tile = jnp.where(lane // count == part, held, tile)
            col_tiles.append(tile)
        for part in range(cols_n):
            held = geo_by_col[(my_col - part + cols_n) % cols_n]
            square_tile = jnp.concatenate(
                [held, jnp.zeros((LANES - 8, LANES), jnp.float32)], axis=0
            )
            row_geo[part] = square_tile.T

        @pl.loop(0, row_span // count)
        def _(part):
            def at_row_point(point, totals):
                start = pl.multiple_of(point * count, 8)
                here = [row_geo[part, pl.ds(start + first, 8), :] for first in range(0, count, 8)]
                spread = [
                    [jnp.broadcast_to(one[:, comp : comp + 1], (8, LANES)) for comp in range(4)]
                    for one in here
                ]
                totals = list(totals)
                for tile in col_tiles:
                    bx, by, bz, bw = (tile[comp : comp + 1] for comp in range(4))
                    for piece, (ax, ay, az, aw) in enumerate(spread):
                        xx, yy, xy, xz, yz, near, soft = totals[piece]
                        dx = ax - bx
                        dy = ay - by
                        dz = az - bz
                        inverse = lax.rsqrt(dx * dx + dy * dy + (dz * dz + EPS_SQUARED))
                        scaled = aw * bw * inverse
                        cubed = scaled * (inverse * inverse)
                        ex = cubed * dx
                        ey = cubed * dy
                        totals[piece] = (
                            xx + ex * dx,
                            yy + ey * dy,
                            xy + ex * dy,
                            xz + ex * dz,
                            yz + ey * dz,
                            near + scaled,
                            soft + cubed,
                        )
                return tuple(totals)

            zero = jnp.zeros((8, LANES), jnp.float32)
            totals = lax.fori_loop(
                0, points, at_row_point, ((zero,) * 7,) * (count // 8), unroll=True
            )
            for piece, (xx, yy, xy, xz, yz, near, soft) in enumerate(totals):
                zz = near - EPS_SQUARED * soft - xx - yy
                even = ISO_TERM * near + SOFT_TERM * soft
                xy, xz, yz = (ANI_TERM * term for term in (xy, xz, yz))
                xx, yy, zz = (ANI_TERM * term + even for term in (xx, yy, zz))
                for line, entry in enumerate((xx, xy, xz, xy, yy, yz, xz, yz, zz)):
                    start = line // 3 * (row_span * 3) + part * (count * 3) + piece * 24 + line % 3
                    out_ref[pl.ds(start, 8, stride=3), :] = entry

    lots = GROUP * SLOTS
    tiles_n = cols_n * rows_n
    acc[...] = jnp.zeros_like(acc)
    small[1] = jnp.zeros_like(small[1])
    number[1] = jnp.zeros_like(number[1])
    down = iota((count, LANES), 0).astype(jnp.float32)
    same = iota((count, lots * count), 1) % count == iota((count, lots * count), 0)
    mine_shape = (PAIR * SLOTS, PAIR * SLOTS * count)
    mine = iota(mine_shape, 0) == iota(mine_shape, 1) // count

    def arrived(first, records_n, sem):
        rows = pl.ds(pl.multiple_of(first * RECORD, 8), records_n * RECORD)
        other = me ^ 1
        return pltpu.make_async_remote_copy(
            src_ref=send.at[rows, :],
            dst_ref=recv.at[rows, :],
            send_sem=send_sem.at[0],
            recv_sem=sem,
            device_id=(other // cols_n, other % cols_n),
            device_id_type=MESH,
        )

    few = PAIR * SLOTS

    def squeeze(batch, turn):
        for part in range(GROUP // PAIR):
            first = batch * GROUP + part * PAIR
            sem = recv_sem.at[first // PAIR]
            if turn or part:
                arrived(first, PAIR, sem).wait_recv()
            else:
                pl.when(batch > 0)(lambda: arrived(first, PAIR, sem).wait_recv())
                pl.when(batch == 0)(lambda: arrived(1, PAIR - 1, sem).wait_recv())
            records = recv.at[pl.ds(pl.multiple_of(first * RECORD, 8), PAIR * RECORD), :]
            place = jnp.concatenate(
                [
                    records[inside * RECORD + SLOTS * COMPS : (inside + 1) * RECORD]
                    for inside in range(PAIR)
                ],
                axis=0,
            )
            whole = jnp.floor(place * (1.0 / (count * count)))
            inner = place - whole * (count * count)
            row_inner = jnp.floor(inner * (1.0 / count))
            column_inner = inner - row_inner * count
            lanes = slice(part * few * count, (part + 1) * few * count)
            number[turn, :, lanes] = jnp.broadcast_to(
                jnp.sum(jnp.where(mine, whole[:, 0:1], 0.0), axis=0, keepdims=True),
                (8, few * count),
            )
            for slot in range(few):
                line = slot // SLOTS * RECORD + slot % SLOTS * COMPS
                at = part * few + slot
                hit = jnp.where(row_inner[slot : slot + 1] == down, 1.0, 0.0).astype(jnp.bfloat16)
                spot = jnp.where(column_inner[slot : slot + 1] == down, 1.0, 0.0).astype(
                    jnp.bfloat16
                )
                for comp in range(COMPS):
                    top, rest = split(
                        jnp.broadcast_to(records[line + comp : line + comp + 1], (count, LANES))
                    )
                    span = slice(comp * count, (comp + 1) * count)
                    left[turn, at, span, :LANES] = hit * top
                    left[turn, at, span, LANES:] = hit * rest.astype(jnp.bfloat16)
                both = jnp.concatenate([spot, spot], axis=1)
                small[turn, at * count : (at + 1) * count] = dot(
                    both, left[turn, at], ((1,), (1,)), None
                )

    def settle(turn):
        top, rest = split(small[turn])
        named = jnp.where(same, jnp.broadcast_to(number[turn, 0:1], same.shape), -1.0)
        for tile in range(tiles_n):
            tiles[tile * count : (tile + 1) * count] = jnp.where(
                named == float(tile), 1.0, 0.0
            ).astype(jnp.bfloat16)
        acc[...] += dot(tiles[...], top, ((1,), (0,)), None) + dot(
            tiles[...], rest.astype(jnp.bfloat16), ((1,), (0,)), None
        )

    @pl.loop(0, devices // GROUP // 2)
    def _(pair):
        pl.when(pair == devices // GROUP // 8)(kelvin)
        settle(1)
        squeeze(pair * 2, 0)
        settle(0)
        squeeze(pair * 2 + 1, 1)

    arrived(1, devices - 1, recv_sem.at[0]).wait_send()
    settle(1)
    most = LANES // count
    for first in range(0, cols_n, most):
        parts = range(first, min(first + most, cols_n))
        last = [acc[part * LANES : (part + 1) * LANES, LANES:] for part in parts]
        gap = LANES - len(last) * count
        if gap:
            last.append(jnp.zeros((LANES, gap), jnp.float32))
        last = jnp.concatenate(last, axis=1).T
        for part in parts:
            main = acc[part * LANES : (part + 1) * LANES, :LANES].T
            for line in range(COMPS):
                if line < most:
                    entry = main[line * count : (line + 1) * count]
                else:
                    entry = last[(part - first) * count : (part - first + 1) * count]
                start = line // 3 * (row_span * 3) + part * (count * 3) + line % 3
                spots = pl.ds(start, count, stride=3)
                out_ref[spots, :] = out_ref[spots, :] + entry


def local(rows_n, cols_n, coords, weights, values, rows, columns, owner, used, fill):
    count = coords.shape[-1]
    devices = rows_n * cols_n
    row_span = cols_n * count
    live_slots = rows.shape[2]
    slots = (live_slots + 15) // 16 * 16
    lots = GROUP * SLOTS
    dma = pltpu.SemaphoreType.DMA
    operands = (
        coords,
        weights,
        values.reshape(-1, 1, LANES),
        rows.reshape(-1, 1, LANES),
        columns.reshape(-1, 1, LANES),
        owner,
        used,
        fill,
    )
    out = pl.pallas_call(
        functools.partial(kernel, rows_n, cols_n),
        out_shape=jax.ShapeDtypeStruct((3 * row_span * 3, LANES), jnp.float32),
        in_specs=[
            pl.BlockSpec(memory_space=pltpu.SMEM if one is used else pltpu.HBM) for one in operands
        ],
        out_specs=pl.BlockSpec(memory_space=pltpu.VMEM),
        scratch_shapes=[
            pltpu.VMEM(coords.shape, jnp.float32),
            pltpu.VMEM(weights.shape, jnp.float32),
            pltpu.VMEM((slots * COMPS, LANES), jnp.float32),
            pltpu.VMEM((slots, LANES), jnp.int32),
            pltpu.VMEM((slots, LANES), jnp.int32),
            pltpu.VMEM(owner.shape, jnp.int32),
            pltpu.VMEM(fill.shape, jnp.int32),
            pltpu.VMEM((devices * RECORD, LANES), jnp.float32),
            pltpu.VMEM((devices * RECORD, LANES), jnp.float32),
            pltpu.VMEM((8, LANES), jnp.float32),
            pltpu.VMEM((rows_n, 8, LANES), jnp.float32),
            pltpu.VMEM((cols_n, 8, LANES), jnp.float32),
            pltpu.VMEM((cols_n, LANES, LANES), jnp.float32),
            pltpu.VMEM((2, lots, COMPS * count, 2 * LANES), jnp.bfloat16),
            pltpu.VMEM((2, lots * count, COMPS * count), jnp.float32),
            pltpu.VMEM((2, 8, lots * count), jnp.float32),
            pltpu.VMEM((devices * count, lots * count), jnp.bfloat16),
            pltpu.VMEM((devices * count, COMPS * count), jnp.float32),
            dma((len(operands) - 1,)),
            dma((1,)),
            dma((devices // PAIR,)),
            dma((rows_n,)),
            dma((rows_n,)),
            dma((cols_n,)),
            dma((cols_n,)),
        ],
        compiler_params=pltpu.CompilerParams(
            collective_id=0, has_side_effects=True, vmem_limit_bytes=40 * 1024 * 1024
        ),
    )(
        *(
            one if one is used else pltpu.with_memory_space_constraint(one, pltpu.HBM)
            for one in operands
        )
    )
    return out.reshape(1, 3, row_span, 3, 1, LANES)


def solution(mesh):
    placed = (
        P("col", "row", None, None, None),
        P("col", "row", None, None),
        P("row", "col", None, None, None),
        P("row", "col", None, None),
        P("row", "col", None, None),
        P("row", "col", None),
        P("row", "col"),
        P("row", "col", None),
    )
    return jax.shard_map(
        functools.partial(local, mesh.shape["row"], mesh.shape["col"]),
        mesh=mesh,
        in_specs=placed,
        out_specs=P("row", None, None, None, "col", None),
        check_vma=False,
    )
```

```python
import functools
import math

import jax
import jax.numpy as jnp
from jax import lax
from jax.experimental import pallas as pl
from jax.experimental.pallas import tpu as pltpu
from jax.sharding import PartitionSpec as P

MESH = pl.DeviceIdType.MESH
HIGH = lax.Precision.HIGHEST
CAP = 2
COMPS = 9
SLOTS = 2 * CAP
RECORD = SLOTS * (COMPS + 1)
LANES = 128
GROUP = 4
PAIR = 2

EPS_SQUARED = 0.01
KELVIN_A = 1.0 / (4.0 * math.pi)
KELVIN_B = KELVIN_A / 2.8
ISO_TERM = KELVIN_A - KELVIN_B
SOFT_TERM = KELVIN_A * 0.005
ANI_TERM = KELVIN_B


def dot(a, b, axes, precision=HIGH):
    return lax.dot_general(
        a, b, (axes, ((), ())), precision=precision, preferred_element_type=jnp.float32
    )


def split(value):
    top = value.astype(jnp.bfloat16)
    return top, value - top.astype(jnp.float32)


def halves(value):
    high, rest = split(value)
    return jnp.concatenate([high, rest.astype(jnp.bfloat16)], axis=0)


def iota(shape, axis):
    return lax.broadcasted_iota(jnp.int32, shape, axis)


def kernel(
    rows_n,
    cols_n,
    coords_hbm,
    weights_hbm,
    values_hbm,
    rows_hbm,
    columns_hbm,
    owner_hbm,
    used_ref,
    fill_hbm,
    out_ref,
    coords_ref,
    weights_ref,
    values_ref,
    rows_ref,
    columns_ref,
    owner_ref,
    fill_ref,
    send,
    recv,
    geo,
    geo_by_row,
    geo_by_col,
    row_geo,
    left,
    small,
    number,
    tiles,
    acc,
    load_sem,
    send_sem,
    recv_sem,
    row_send_sem,
    row_recv_sem,
    col_send_sem,
    col_recv_sem,
):
    my_row = lax.axis_index("row")
    my_col = lax.axis_index("col")
    devices = rows_n * cols_n
    me = my_row * cols_n + my_col
    points, count = coords_ref.shape[-2:]
    row_span = cols_n * count
    live_slots, _, width = rows_hbm.shape
    slots = rows_ref.shape[0]

    barrier = pltpu.get_barrier_semaphore()

    @pl.loop(1, devices, unroll=True)
    def _(k):
        other = me ^ (devices - k)
        pl.semaphore_signal(
            barrier,
            inc=1,
            device_id=(other // cols_n, other % cols_n),
            device_id_type=MESH,
        )

    lines_n = live_slots * COMPS
    loads = [
        pltpu.make_async_copy(source, target, load_sem.at[k])
        for k, (source, target) in enumerate(
            (
                (coords_hbm, coords_ref),
                (weights_hbm, weights_ref),
                (values_hbm.at[:, 0], values_ref.at[pl.ds(0, lines_n)]),
                (rows_hbm.at[:, 0], rows_ref.at[pl.ds(0, live_slots)]),
                (columns_hbm.at[:, 0], columns_ref.at[pl.ds(0, live_slots)]),
                (owner_hbm, owner_ref),
                (fill_hbm, fill_ref),
            )
        )
    ]
    edge = live_slots // 8 * 8
    rows_ref[edge:slots] = jnp.zeros((slots - edge, width), jnp.int32)
    columns_ref[edge:slots] = jnp.zeros((slots - edge, width), jnp.int32)
    edge = lines_n // 8 * 8
    values_ref[edge : slots * COMPS] = jnp.zeros((slots * COMPS - edge, width), jnp.float32)
    for load in loads:
        load.start()

    for load in loads[:2]:
        load.wait()
    spread = (iota((count, LANES), 1) % count == iota((count, LANES), 0)).astype(jnp.float32)
    at_point = iota((points, LANES), 1) // count == iota((points, LANES), 0)
    lines = []
    for comp in range(4):
        piece = coords_ref[0, 0, comp] if comp < 3 else weights_ref[0, 0]
        wide = dot(piece, spread, ((1,), (0,)))
        lines.append(jnp.sum(jnp.where(at_point, wide, 0.0), axis=0, keepdims=True))
    geo[...] = jnp.concatenate(lines + [jnp.zeros((4, LANES), jnp.float32)], axis=0)
    geo_by_col[0] = geo[...]
    geo_by_row[0] = geo[...]

    def row_copy(k):
        return pltpu.make_async_remote_copy(
            src_ref=geo,
            dst_ref=geo_by_row.at[k],
            send_sem=row_send_sem.at[k],
            recv_sem=row_recv_sem.at[k],
            device_id=((my_row + k) % rows_n, my_col),
            device_id_type=MESH,
        )

    def col_copy(k):
        return pltpu.make_async_remote_copy(
            src_ref=geo,
            dst_ref=geo_by_col.at[k],
            send_sem=col_send_sem.at[k],
            recv_sem=col_recv_sem.at[k],
            device_id=(my_row, (my_col + k) % cols_n),
            device_id_type=MESH,
        )

    for load in loads[2:]:
        load.wait()
    owner = jnp.concatenate([owner_ref[0], jnp.zeros((1, slots - live_slots), jnp.int32)], axis=1)
    fills = jnp.concatenate([fill_ref[0], jnp.zeros((1, slots - live_slots), jnp.int32)], axis=1)
    live = iota((1, slots), 1) < used_ref[0, 0]
    square = (slots, slots)
    diagonal = iota(square, 0) == iota(square, 1)
    fill = jnp.sum(jnp.where(diagonal, fills, 0), axis=1, keepdims=True)
    owner_down = jnp.sum(jnp.where(diagonal, owner, 0), axis=1, keepdims=True)
    row_position = rows_ref[...]
    column_position = columns_ref[...]
    row_group = row_position[:, 0:1] // count
    column_group = column_position[:, 0:1] // count
    mirror_down = column_group * cols_n + row_group
    mirror = jnp.sum(jnp.where(diagonal, mirror_down, 0), axis=0, keepdims=True)
    earlier = (iota(square, 0) < iota(square, 1)).astype(jnp.float32).astype(jnp.bfloat16)
    picks = []
    for target in (owner, mirror):
        named = ((target == iota((devices, slots), 0)) & live).astype(jnp.float32)
        rank = dot(named.astype(jnp.bfloat16), earlier, ((1,), (0,)), None)
        for place in range(CAP):
            picks.append(jnp.where(rank == float(place), named, 0.0))
    pick = jnp.concatenate(picks, axis=0).astype(jnp.bfloat16)
    pick = jnp.concatenate([pick, pick], axis=1)
    valid = iota((slots, width), 1) < fill
    row_inner = row_position % count
    column_inner = column_position % count
    forward = ((row_group * rows_n + column_group) * count + row_inner) * count + column_inner
    back_tile = owner_down % cols_n * rows_n + owner_down // cols_n
    backward = (back_tile * count + column_inner) * count + row_inner
    half = CAP * devices
    places = (
        dot(pick[:half], halves(forward.astype(jnp.float32)), ((1,), (0,)), None),
        dot(pick[half:], halves(backward.astype(jnp.float32)), ((1,), (0,)), None),
    )
    for slot in range(SLOTS):
        lot = places[slot // CAP][slot % CAP * devices : (slot % CAP + 1) * devices]
        send[pl.ds(SLOTS * COMPS + slot, devices, stride=RECORD), :] = lot
    for comp in range(COMPS):
        value = values_ref[pl.ds(comp, slots, stride=COMPS), :]
        sent = dot(pick, halves(jnp.where(valid, value, 0.0)), ((1,), (0,)), None)
        for slot in range(SLOTS):
            line = comp if slot < CAP else comp % 3 * 3 + comp // 3
            send[pl.ds(slot * COMPS + line, devices, stride=RECORD), :] = sent[
                slot * devices : (slot + 1) * devices
            ]

    pl.semaphore_wait(barrier, devices - 1)
    for k in range(1, cols_n):
        col_copy(k).start()
    for k in range(1, rows_n):
        row_copy(k).start()
    recv[0:RECORD, :] = send[pl.ds(pl.multiple_of(me * RECORD, 8), RECORD), :]

    def block_copy(k):
        other = me ^ k
        return pltpu.make_async_remote_copy(
            src_ref=send.at[pl.ds(pl.multiple_of(other * RECORD, 8), RECORD), :],
            dst_ref=recv.at[pl.ds(pl.multiple_of(k * RECORD, 8), RECORD), :],
            send_sem=send_sem.at[0],
            recv_sem=recv_sem.at[k // PAIR],
            device_id=(other // cols_n, other % cols_n),
            device_id_type=MESH,
        )

    for k in range(1, devices):
        block_copy(k if k < 2 else k ^ 1).start()

    def kelvin():
        pl.loop(1, cols_n)(lambda k: col_copy(k).wait())
        pl.loop(1, rows_n)(lambda k: row_copy(k).wait())

        lane = iota((8, LANES), 1)
        col_tiles = []
        for point in range(points):
            tile = jnp.zeros((8, LANES), jnp.float32)
            for part in range(rows_n):
                held = geo_by_row[(my_row - part + rows_n) % rows_n]
                shift = (part - point) * count % LANES
                if shift:
                    held = pltpu.roll(held, shift, 1)
                tile = jnp.where(lane // count == part, held, tile)
            col_tiles.append(tile)
        for part in range(cols_n):
            held = geo_by_col[(my_col - part + cols_n) % cols_n]
            square_tile = jnp.concatenate(
                [held, jnp.zeros((LANES - 8, LANES), jnp.float32)], axis=0
            )
            row_geo[part] = square_tile.T

        @pl.loop(0, row_span // count)
        def _(part):
            def at_row_point(point, totals):
                start = pl.multiple_of(point * count, 8)
                here = [row_geo[part, pl.ds(start + first, 8), :] for first in range(0, count, 8)]
                spread = [
                    [jnp.broadcast_to(one[:, comp : comp + 1], (8, LANES)) for comp in range(4)]
                    for one in here
                ]
                totals = list(totals)
                for tile in col_tiles:
                    bx, by, bz, bw = (tile[comp : comp + 1] for comp in range(4))
                    for piece, (ax, ay, az, aw) in enumerate(spread):
                        xx, yy, xy, xz, yz, near, soft = totals[piece]
                        dx = ax - bx
                        dy = ay - by
                        dz = az - bz
                        inverse = lax.rsqrt(dx * dx + dy * dy + (dz * dz + EPS_SQUARED))
                        scaled = aw * bw * inverse
                        cubed = scaled * (inverse * inverse)
                        ex = cubed * dx
                        ey = cubed * dy
                        totals[piece] = (
                            xx + ex * dx,
                            yy + ey * dy,
                            xy + ex * dy,
                            xz + ex * dz,
                            yz + ey * dz,
                            near + scaled,
                            soft + cubed,
                        )
                return tuple(totals)

            zero = jnp.zeros((8, LANES), jnp.float32)
            totals = lax.fori_loop(
                0, points, at_row_point, ((zero,) * 7,) * (count // 8), unroll=True
            )
            for piece, (xx, yy, xy, xz, yz, near, soft) in enumerate(totals):
                zz = near - EPS_SQUARED * soft - xx - yy
                even = ISO_TERM * near + SOFT_TERM * soft
                xy, xz, yz = (ANI_TERM * term for term in (xy, xz, yz))
                xx, yy, zz = (ANI_TERM * term + even for term in (xx, yy, zz))
                for line, entry in enumerate((xx, xy, xz, xy, yy, yz, xz, yz, zz)):
                    start = line // 3 * (row_span * 3) + part * (count * 3) + piece * 24 + line % 3
                    out_ref[pl.ds(start, 8, stride=3), :] = entry

    lots = GROUP * SLOTS
    tiles_n = cols_n * rows_n
    acc[...] = jnp.zeros_like(acc)
    down = iota((count, LANES), 0).astype(jnp.float32)
    same = iota((count, lots * count), 1) % count == iota((count, lots * count), 0)
    mine_shape = (PAIR * SLOTS, PAIR * SLOTS * count)
    mine = iota(mine_shape, 0) == iota(mine_shape, 1) // count

    def arrived(first, records_n, sem):
        rows = pl.ds(pl.multiple_of(first * RECORD, 8), records_n * RECORD)
        other = me ^ 1
        return pltpu.make_async_remote_copy(
            src_ref=send.at[rows, :],
            dst_ref=recv.at[rows, :],
            send_sem=send_sem.at[0],
            recv_sem=sem,
            device_id=(other // cols_n, other % cols_n),
            device_id_type=MESH,
        )

    few = PAIR * SLOTS

    def squeeze(batch, turn):
        for part in range(GROUP // PAIR):
            first = batch * GROUP + part * PAIR
            sem = recv_sem.at[first // PAIR]
            if turn or part:
                arrived(first, PAIR, sem).wait_recv()
            else:
                pl.when(batch > 0)(lambda: arrived(first, PAIR, sem).wait_recv())
                pl.when(batch == 0)(lambda: arrived(1, PAIR - 1, sem).wait_recv())
            records = recv.at[pl.ds(pl.multiple_of(first * RECORD, 8), PAIR * RECORD), :]
            place = jnp.concatenate(
                [
                    records[inside * RECORD + SLOTS * COMPS : (inside + 1) * RECORD]
                    for inside in range(PAIR)
                ],
                axis=0,
            )
            whole = jnp.floor(place * (1.0 / (count * count)))
            inner = place - whole * (count * count)
            row_inner = jnp.floor(inner * (1.0 / count))
            column_inner = inner - row_inner * count
            lanes = slice(part * few * count, (part + 1) * few * count)
            number[turn, :, lanes] = jnp.broadcast_to(
                jnp.sum(jnp.where(mine, whole[:, 0:1], 0.0), axis=0, keepdims=True),
                (8, few * count),
            )
            for slot in range(few):
                line = slot // SLOTS * RECORD + slot % SLOTS * COMPS
                at = part * few + slot
                hit = jnp.where(row_inner[slot : slot + 1] == down, 1.0, 0.0).astype(jnp.bfloat16)
                spot = jnp.where(column_inner[slot : slot + 1] == down, 1.0, 0.0).astype(
                    jnp.bfloat16
                )
                for comp in range(COMPS):
                    top, rest = split(
                        jnp.broadcast_to(records[line + comp : line + comp + 1], (count, LANES))
                    )
                    span = slice(comp * count, (comp + 1) * count)
                    left[turn, at, span, :LANES] = hit * top
                    left[turn, at, span, LANES:] = hit * rest.astype(jnp.bfloat16)
                both = jnp.concatenate([spot, spot], axis=1)
                small[turn, at * count : (at + 1) * count] = dot(
                    both, left[turn, at], ((1,), (1,)), None
                )

    def settle(turn):
        top, rest = split(small[turn])
        named = jnp.where(same, jnp.broadcast_to(number[turn, 0:1], same.shape), -1.0)
        for tile in range(tiles_n):
            tiles[tile * count : (tile + 1) * count] = jnp.where(
                named == float(tile), 1.0, 0.0
            ).astype(jnp.bfloat16)
        acc[...] += dot(tiles[...], top, ((1,), (0,)), None) + dot(
            tiles[...], rest.astype(jnp.bfloat16), ((1,), (0,)), None
        )

    @pl.loop(0, devices // GROUP // 2)
    def _(pair):
        pl.when(pair == devices // GROUP // 8)(kelvin)
        pl.when(pair > 0)(lambda: settle(1))
        squeeze(pair * 2, 0)
        settle(0)
        squeeze(pair * 2 + 1, 1)

    arrived(1, devices - 1, recv_sem.at[0]).wait_send()
    settle(1)
    most = LANES // count
    for first in range(0, cols_n, most):
        parts = range(first, min(first + most, cols_n))
        last = [acc[part * LANES : (part + 1) * LANES, LANES:] for part in parts]
        gap = LANES - len(last) * count
        if gap:
            last.append(jnp.zeros((LANES, gap), jnp.float32))
        last = jnp.concatenate(last, axis=1).T
        for part in parts:
            main = acc[part * LANES : (part + 1) * LANES, :LANES].T
            for line in range(COMPS):
                if line < most:
                    entry = main[line * count : (line + 1) * count]
                else:
                    entry = last[(part - first) * count : (part - first + 1) * count]
                start = line // 3 * (row_span * 3) + part * (count * 3) + line % 3
                spots = pl.ds(start, count, stride=3)
                out_ref[spots, :] = out_ref[spots, :] + entry


def local(rows_n, cols_n, coords, weights, values, rows, columns, owner, used, fill):
    count = coords.shape[-1]
    devices = rows_n * cols_n
    row_span = cols_n * count
    live_slots = rows.shape[2]
    slots = (live_slots + 15) // 16 * 16
    lots = GROUP * SLOTS
    dma = pltpu.SemaphoreType.DMA
    operands = (
        coords,
        weights,
        values.reshape(-1, 1, LANES),
        rows.reshape(-1, 1, LANES),
        columns.reshape(-1, 1, LANES),
        owner,
        used,
        fill,
    )
    out = pl.pallas_call(
        functools.partial(kernel, rows_n, cols_n),
        out_shape=jax.ShapeDtypeStruct((3 * row_span * 3, LANES), jnp.float32),
        in_specs=[
            pl.BlockSpec(memory_space=pltpu.SMEM if one is used else pltpu.HBM) for one in operands
        ],
        out_specs=pl.BlockSpec(memory_space=pltpu.VMEM),
        scratch_shapes=[
            pltpu.VMEM(coords.shape, jnp.float32),
            pltpu.VMEM(weights.shape, jnp.float32),
            pltpu.VMEM((slots * COMPS, LANES), jnp.float32),
            pltpu.VMEM((slots, LANES), jnp.int32),
            pltpu.VMEM((slots, LANES), jnp.int32),
            pltpu.VMEM(owner.shape, jnp.int32),
            pltpu.VMEM(fill.shape, jnp.int32),
            pltpu.VMEM((devices * RECORD, LANES), jnp.float32),
            pltpu.VMEM((devices * RECORD, LANES), jnp.float32),
            pltpu.VMEM((8, LANES), jnp.float32),
            pltpu.VMEM((rows_n, 8, LANES), jnp.float32),
            pltpu.VMEM((cols_n, 8, LANES), jnp.float32),
            pltpu.VMEM((cols_n, LANES, LANES), jnp.float32),
            pltpu.VMEM((2, lots, COMPS * count, 2 * LANES), jnp.bfloat16),
            pltpu.VMEM((2, lots * count, COMPS * count), jnp.float32),
            pltpu.VMEM((2, 8, lots * count), jnp.float32),
            pltpu.VMEM((devices * count, lots * count), jnp.bfloat16),
            pltpu.VMEM((devices * count, COMPS * count), jnp.float32),
            dma((len(operands) - 1,)),
            dma((1,)),
            dma((devices // PAIR,)),
            dma((rows_n,)),
            dma((rows_n,)),
            dma((cols_n,)),
            dma((cols_n,)),
        ],
        compiler_params=pltpu.CompilerParams(
            collective_id=0, has_side_effects=True, vmem_limit_bytes=40 * 1024 * 1024
        ),
    )(
        *(
            one if one is used else pltpu.with_memory_space_constraint(one, pltpu.HBM)
            for one in operands
        )
    )
    return out.reshape(1, 3, row_span, 3, 1, LANES)


def solution(mesh):
    placed = (
        P("col", "row", None, None, None),
        P("col", "row", None, None),
        P("row", "col", None, None, None),
        P("row", "col", None, None),
        P("row", "col", None, None),
        P("row", "col", None),
        P("row", "col"),
        P("row", "col", None),
    )
    return jax.shard_map(
        functools.partial(local, mesh.shape["row"], mesh.shape["col"]),
        mesh=mesh,
        in_specs=placed,
        out_specs=P("row", None, None, None, "col", None),
        check_vma=False,
    )
```
